256 devices in a mesh: dp: 8 (over y, core), ctx: 32 (over x, z).
Axes of the slice: x: 4, y: 4, z: 8, core: 2. Of those that a mesh axis runs over, the one named last changes fastest.
Arguments:
- query_act: bfloat16 [32768, 4096], P(('dp', 'ctx')), may hold values from -6 to 6
- key_act: bfloat16 [32768, 4096], P(('dp', 'ctx')), may hold values from -6 to 6
- value_act: bfloat16 [32768, 4096], P(('dp', 'ctx')), may hold values from -6 to 6
- out_grad: bfloat16 [32768, 4096], P(('dp', 'ctx')), may hold values from -6 to 6
- filter_taps: float32 [4096, 128], P('ctx'), may hold values from -0.5 to 0.5
- doc_ids: int32 [32768], replicated, may hold values from 0 to 7, as said below
Outputs:
- query_grad: bfloat16 [32768, 4096], P(('dp', 'ctx'))
- key_grad: bfloat16 [32768, 4096], P(('dp', 'ctx'))
- value_grad: bfloat16 [32768, 4096], P(('dp', 'ctx'))
- filter_grad: float32 [4096, 128], P('ctx')
The draws below stay inside these ranges and needn't reach their ends.
Inputs may be any that keep to these rules, and one draw needn't show every extreme that they name: `doc_ids`: the document numbers start at 0, never fall, and rise by one at each boundary; the window holds 8 documents, each of at least 256 positions.
All inputs are finite; a program needn't handle non-finite values.
Results may differ from the reference program's by a relative error of at most 0.0064.
Values may be sent and summed in bfloat16 or wider, within the bound.
A program may use at most 192 MiB of HBM per device.

```python
import math
import jax
import jax.numpy as jnp
from jax import lax

D = 4096
FL = 128
DOCS = 8
SEQ_LEN = 32768


def draw_doc_ids(key, part):
    spare_rows = SEQ_LEN - DOCS * 2 * FL
    cut_points = jnp.sort(jax.random.randint(key, (DOCS - 1,), 0, spare_rows + 1))
    starts = cut_points + 2 * FL * jnp.arange(1, DOCS, dtype=jnp.int32)
    positions = jnp.arange(SEQ_LEN, dtype=jnp.int32)
    marks = (positions[:, None] >= starts[None, :]).astype(jnp.int32)
    return jnp.sum(marks, axis=1).astype(jnp.int32)


def steps_of(key, extent, split, low, high):
    loudness = 1.0
    for position, blocks in split:
        steps = jax.random.uniform(jax.random.fold_in(jax.random.fold_in(key, 6), position), (blocks,), jnp.float32, low / len(split), high / len(split))
        loudness = loudness * jnp.repeat(jnp.exp(steps), extent[position] // blocks).reshape((-1,) + (1,) * (len(extent) - 1 - position))
    return loudness


def normal_values(rng, dims, scale, reach, split=(), held_as=jnp.bfloat16):
    array = scale * jax.random.normal(rng, dims, jnp.float32)
    if split:
        array = array * steps_of(rng, dims, split, -0.22, 0.18)
    return jnp.clip(array, -reach, reach).astype(held_as)


def setup_inputs(seed: int = 0) -> dict:
    seeds = jax.random.split(jax.random.key(seed), 7)
    query_act = normal_values(seeds[0], (SEQ_LEN, D), 1.0, 6.0, ((0, 256),))
    key_act = normal_values(seeds[1], (SEQ_LEN, D), 1.0, 6.0, ((0, 256),))
    value_act = normal_values(seeds[2], (SEQ_LEN, D), 1.0, 6.0, ((0, 256),))
    out_grad = normal_values(seeds[3], (SEQ_LEN, D), 1.0, 6.0, ((0, 256),))
    filter_taps = normal_values(seeds[4], (D, FL), FL ** -0.5, 0.5, ((0, 32),), jnp.float32)
    doc_ids = draw_doc_ids(jax.random.fold_in(seeds[6], 71), 0)
    return dict(query_act=query_act, key_act=key_act, value_act=value_act, out_grad=out_grad, filter_taps=filter_taps, doc_ids=doc_ids)


def build_toeplitz(tap_rows):
    chan_count, tap_count = tap_rows.shape
    zero_col = jnp.zeros((chan_count, 1), tap_rows.dtype)
    tail_cols = jnp.zeros((chan_count, tap_count), tap_rows.dtype)
    pattern = jnp.concatenate([zero_col, tap_rows[:, ::-1], tail_cols], axis=1)
    tiled = jnp.tile(pattern, (1, tap_count))[:, :tap_count * 2 * tap_count]
    return tiled.reshape(chan_count, tap_count, 2 * tap_count)

def lag_sums(block):
    chan_count, tap_count, span = block.shape
    flat = block.reshape(chan_count, tap_count * span)
    flat = jnp.pad(flat, ((0, 0), (0, tap_count)))
    skewed = flat.reshape(chan_count, tap_count, span + 1)
    summed = lax.optimization_barrier(jnp.sum(skewed[:, :, 1:tap_count + 1], axis=1))
    return summed[:, ::-1]

def mix_exact(kv_ext, g_ext, seg_ext, tap_rows):
    chan_count, tap_count = tap_rows.shape
    block_count = kv_ext.shape[1] // tap_count - 1
    kv_blocks = kv_ext.reshape(chan_count, block_count + 1, tap_count)
    windows = jnp.concatenate([kv_blocks[:, :-1], kv_blocks[:, 1:]], axis=2)
    seg_blocks = seg_ext.reshape(block_count + 2, tap_count)
    seg_win = jnp.concatenate([seg_blocks[:-1], seg_blocks[1:]], axis=1)
    same = (seg_win == seg_win[:, -1:]).astype(jnp.float32)
    other = 1.0 - same
    rows_same = same[:, tap_count:]
    rows_other = other[:, tap_count:]
    toeplitz = build_toeplitz(tap_rows)
    kv_same = same[:block_count] * windows
    kv_other = other[:block_count] * windows
    z_same = jnp.einsum('cij,cbj->cbi', toeplitz, kv_same, precision=lax.Precision.HIGHEST)
    z_other = jnp.einsum('cij,cbj->cbi', toeplitz, kv_other, precision=lax.Precision.HIGHEST)
    mixed = rows_same[:block_count] * z_same + rows_other[:block_count] * z_other
    g_blocks = g_ext.reshape(chan_count, block_count + 1, tap_count)
    g_same = rows_same * g_blocks
    g_other = rows_other * g_blocks
    d_same = jnp.einsum('cij,cbi->cbj', toeplitz, g_same, precision=lax.Precision.HIGHEST)
    d_other = jnp.einsum('cij,cbi->cbj', toeplitz, g_other, precision=lax.Precision.HIGHEST)
    d_win = same * d_same + other * d_other
    back = d_win[:, :block_count, tap_count:] + d_win[:, 1:, :tap_count]
    outer = jnp.einsum('cbi,cbj->cij', g_same[:, :block_count], kv_same, precision=lax.Precision.HIGHEST)
    outer = outer + jnp.einsum('cbi,cbj->cij', g_other[:, :block_count], kv_other, precision=lax.Precision.HIGHEST)
    row_count = block_count * tap_count
    return (mixed.reshape(chan_count, row_count), back.reshape(chan_count, row_count), lag_sums(outer))

def reference(query_act, key_act, value_act, out_grad, filter_taps, doc_ids):
    tap_count = filter_taps.shape[1]
    chan_count = filter_taps.shape[0]
    product = lax.optimization_barrier((key_act.astype(jnp.float32) * value_act.astype(jnp.float32)).astype(jnp.bfloat16))
    gated = lax.optimization_barrier((query_act.astype(jnp.float32) * out_grad.astype(jnp.float32)).astype(jnp.bfloat16))
    taps = lax.optimization_barrier(filter_taps.astype(jnp.bfloat16)).astype(jnp.float32)
    width = math.gcd(chan_count, 512)
    group_count = chan_count // width
    taps_groups = taps.reshape(group_count, width, tap_count)
    row_count = product.shape[0]
    kv_ext = jnp.concatenate([jnp.zeros((tap_count, chan_count), jnp.bfloat16), product], 0).T
    g_ext = jnp.concatenate([gated, jnp.zeros((tap_count, chan_count), jnp.bfloat16)], 0).T
    seg_ext = jnp.pad(doc_ids, (tap_count, tap_count))
    kv_groups = kv_ext.reshape(group_count, width, row_count + tap_count)
    g_groups = g_ext.reshape(group_count, width, row_count + tap_count)

    def one_group(parts):
        return mix_exact(parts[0].astype(jnp.float32), parts[1].astype(jnp.float32), seg_ext, parts[2])
    mixed, back, partial_value = lax.map(one_group, (kv_groups, g_groups, taps_groups))
    mixed = mixed.reshape(chan_count, row_count).T
    back = back.reshape(chan_count, row_count).T
    mixed = lax.optimization_barrier(mixed.astype(jnp.bfloat16)).astype(jnp.float32)
    back = lax.optimization_barrier(back.astype(jnp.bfloat16)).astype(jnp.float32)
    query_grad = (out_grad.astype(jnp.float32) * mixed).astype(jnp.bfloat16)
    key_grad = (back * value_act.astype(jnp.float32)).astype(jnp.bfloat16)
    value_grad = (back * key_act.astype(jnp.float32)).astype(jnp.bfloat16)
    filter_grad = partial_value.reshape(chan_count, tap_count) * (1.0 / math.sqrt(SEQ_LEN))
    return (query_grad, key_grad, value_grad, filter_grad)
```

```python
import functools
import math

import jax
import jax.numpy as jnp
import numpy as np
import ml_dtypes
from jax import lax
from jax.experimental import pallas as pl
from jax.experimental.pallas import tpu as pltpu
from jax.sharding import PartitionSpec as P

FL = 128
BINS = 192
N = 2 * BINS
CHUNK = 256
F32 = jnp.float32
BF16 = jnp.bfloat16


def tables():
    k = np.arange(BINS)[:, None]
    fwd, inv = [], []
    for block in range(3):
        u = np.arange(FL)[None, :] + FL * block
        angle = np.pi * ((2 * k + 1) * u % (2 * N)) / N
        full = np.concatenate([np.cos(angle), np.sin(angle)], 0)
        high = full.astype(ml_dtypes.bfloat16)
        low = (full - high.astype(np.float64)).astype(ml_dtypes.bfloat16)
        fwd.append(np.concatenate([high, low], 1))
        zero = np.zeros_like(low.T)
        inv.append(
            np.concatenate(
                [np.concatenate([high.T, high.T], 1), np.concatenate([low.T, zero], 1)], 0
            )
        )
    return np.stack(fwd), np.stack(inv[:2])


def build_matrices(docs, fwd_tab, inv_tab, e_own, e_prev, e_next, d_own):
    own = docs[1:2, :]
    first, last = own[:, :1], own[:, FL - 1 :]
    moved = (own != first).astype(F32)
    split = (first != last).astype(F32)
    keep_prev = (docs[0:1, :] == first).astype(F32)
    keep_next = (docs[2:3, :] == last).astype(F32)
    twice = lambda row: jnp.concatenate([row, row], 1)
    t0, t1, t2 = (fwd_tab[i].astype(F32) for i in range(3))
    m = twice(moved)
    e_own[...] = (t0 * (1.0 - m) + t1 * m).astype(BF16)
    e_prev[...] = (-t2 * twice(keep_prev)).astype(BF16)
    e_next[...] = ((t1 * (1.0 - split) + t2 * split) * twice(keep_next)).astype(BF16)
    square = jnp.broadcast_to(moved, (FL, FL)).T
    wide = jnp.concatenate([square] * (2 * N // FL), 1)
    for half in range(2):
        rows = pl.ds(half * FL, FL)
        d0, d1 = inv_tab[0, rows, :].astype(F32), inv_tab[1, rows, :].astype(F32)
        d_own[rows, :] = (d0 * (1.0 - wide) + d1 * wide).astype(BF16)


def forward(matrix, block):
    return jnp.dot(
        matrix, jnp.concatenate([block, block], 0), preferred_element_type=F32
    )


def inverse(matrix, cosines, sines):
    spectrum = jnp.concatenate([cosines, sines], 0)
    high = spectrum.astype(BF16)
    low = (spectrum - high.astype(F32)).astype(BF16)
    both = jnp.dot(matrix, jnp.concatenate([high, low], 0), preferred_element_type=F32)
    return both[:FL] + both[FL:]


def convolve(a, b):
    ca, sa, cb, sb = a[:BINS], a[BINS:], b[:BINS], b[BINS:]
    return ca * cb - sa * sb, ca * sb + sa * cb


def correlate(a, b):
    ca, sa, cb, sb = a[:BINS], a[BINS:], b[:BINS], b[BINS:]
    return ca * cb + sa * sb, ca * sb - sa * cb


def kernel(docs, fwd_tab, inv_tab, taps, p, p_prev, g, g_next, k_ref, v_ref, o_ref,
           qg_ref, kg_ref, vg_ref, fg_ref, e_own, e_prev, e_next, d_own):
    @pl.when(pl.program_id(0) == 0)
    def _():
        build_matrices(docs[...], fwd_tab, inv_tab, e_own, e_prev, e_next, d_own)

    h_hat = forward(fwd_tab[0], taps[...])
    p_hat = forward(e_own[...], p[...]) + forward(e_prev[...], p_prev[...])
    g_own = forward(e_own[...], g[...])
    g_hat = g_own + forward(e_next[...], g_next[...])
    fg_ref[...] = inverse(inv_tab[0], *correlate(p_hat, g_own)) * (1.0 / BINS)
    mixed = (inverse(d_own[...], *convolve(h_hat, p_hat)) * (1.0 / BINS)).astype(BF16).astype(F32)
    back = (inverse(d_own[...], *correlate(h_hat, g_hat)) * (1.0 / BINS)).astype(BF16).astype(F32)
    qg_ref[...] = (o_ref[...].astype(F32) * mixed).astype(BF16)
    kg_ref[...] = (back * v_ref[...].astype(F32)).astype(BF16)
    vg_ref[...] = (back * k_ref[...].astype(F32)).astype(BF16)


def shards(query_act, key_act, value_act, out_grad, filter_taps, doc_ids):
    rows, chans = key_act.shape
    count = lax.axis_size("dp") * lax.axis_size("ctx")
    scale = 1.0 / math.sqrt(doc_ids.shape[0])
    product = (key_act.astype(F32) * value_act.astype(F32)).astype(BF16)
    gated = (query_act.astype(F32) * out_grad.astype(F32)).astype(BF16)
    p_prev = lax.ppermute(product, ("dp", "ctx"), [(i, i + 1) for i in range(count - 1)])
    g_next = lax.ppermute(gated, ("dp", "ctx"), [(i + 1, i) for i in range(count - 1)])
    taps = lax.all_gather(filter_taps.astype(BF16).T, "ctx", axis=1, tiled=True)
    me = lax.axis_index("dp") * lax.axis_size("ctx") + lax.axis_index("ctx")
    docs = lax.dynamic_slice_in_dim(
        jnp.pad(doc_ids, (FL, FL), constant_values=-1), me * rows, 3 * FL
    ).reshape(3, FL)
    fwd_tab, inv_tab = tables()
    whole = lambda a: pl.BlockSpec(a.shape, lambda i: (0,) * a.ndim)
    part = pl.BlockSpec((FL, CHUNK), lambda i: (0, i))
    acts = jax.ShapeDtypeStruct((FL, chans), BF16)
    query_grad, key_grad, value_grad, partial_grad = pl.pallas_call(
        kernel,
        grid=(chans // CHUNK,),
        in_specs=[whole(docs), whole(fwd_tab), whole(inv_tab)] + [part] * 8,
        out_specs=[part] * 4,
        out_shape=[acts, acts, acts, jax.ShapeDtypeStruct((FL, chans), F32)],
        scratch_shapes=[
            pltpu.VMEM((N, 2 * FL), BF16),
            pltpu.VMEM((N, 2 * FL), BF16),
            pltpu.VMEM((N, 2 * FL), BF16),
            pltpu.VMEM((2 * FL, 2 * N), BF16),
        ],
        name="mixer",
    )(docs, jnp.asarray(fwd_tab), jnp.asarray(inv_tab), taps, product, p_prev, gated, g_next,
      key_act, value_act, out_grad)
    partial_grad = lax.psum_scatter(partial_grad, "ctx", scatter_dimension=1, tiled=True)
    total = lax.psum(partial_grad, "dp")
    return query_grad, key_grad, value_grad, total.T * scale


def solution(mesh):
    act = P(("dp", "ctx"), None)
    return jax.shard_map(
        shards,
        mesh=mesh,
        in_specs=(act, act, act, act, P("ctx", None), P()),
        out_specs=(act, act, act, P("ctx", None)),
        check_vma=False,
    )
```

```python
import functools
import math

import jax
import jax.numpy as jnp
import numpy as np
import ml_dtypes
from jax import lax
from jax.experimental import pallas as pl
from jax.experimental.pallas import tpu as pltpu
from jax.sharding import PartitionSpec as P

FL = 128
BINS = 192
N = 2 * BINS
CHUNK = 256
F32 = jnp.float32
BF16 = jnp.bfloat16


def tables():
    k = np.arange(BINS)[:, None]
    fwd, inv = [], []
    for block in range(3):
        u = np.arange(FL)[None, :] + FL * block
        angle = np.pi * ((2 * k + 1) * u % (2 * N)) / N
        full = np.concatenate([np.cos(angle), np.sin(angle)], 0)
        high = full.astype(ml_dtypes.bfloat16)
        low = (full - high.astype(np.float64)).astype(ml_dtypes.bfloat16)
        fwd.append(np.concatenate([high, low], 1))
        zero = np.zeros_like(low.T)
        inv.append(
            np.concatenate(
                [np.concatenate([high.T, high.T], 1), np.concatenate([low.T, zero], 1)], 0
            )
        )
    return np.stack(fwd), np.stack(inv[:2])


def forward(matrix, block):
    return jnp.dot(
        matrix, jnp.concatenate([block, block], 0), preferred_element_type=F32
    )


def inverse(matrix, cosines, sines):
    spectrum = jnp.concatenate([cosines, sines], 0)
    high = spectrum.astype(BF16)
    low = (spectrum - high.astype(F32)).astype(BF16)
    both = jnp.dot(matrix, jnp.concatenate([high, low], 0), preferred_element_type=F32)
    return both[:FL] + both[FL:]


def convolve(a, b):
    ca, sa, cb, sb = a[:BINS], a[BINS:], b[:BINS], b[BINS:]
    return ca * cb - sa * sb, ca * sb + sa * cb


def correlate(a, b):
    ca, sa, cb, sb = a[:BINS], a[BINS:], b[:BINS], b[BINS:]
    return ca * cb + sa * sb, ca * sb - sa * cb

MESH = pl.DeviceIdType.MESH


class Layout:
    def __init__(self, dp, ctx, chans, chunk=CHUNK):
        self.dp, self.ctx, self.cores, self.ys = dp, ctx, 2, dp // 2
        self.zs = 8 if ctx == 32 else ctx // 2
        self.xs = ctx // self.zs
        self.chans, self.chunk = chans, chunk
        self.chunks = chans // chunk
        self.half = self.chunks // 2
        self.group = self.chunks // self.xs
        self.rows = FL // dp
        self.lanes = chans // ctx
        self.ahead = min(3, self.half)


def remote(src, dst, send, recv, device):
    return pltpu.make_async_remote_copy(
        src_ref=src, dst_ref=dst, send_sem=send, recv_sem=recv, device_id=device,
        device_id_type=MESH,
    )


def kernel(lay, scale, q_hbm, k_hbm, v_hbm, o_hbm, taps, docs, fwd_tab, inv_tab,
           qg_ref, kg_ref, vg_ref, fg_ref,
           q, k, v, o, p, g, p_prev, g_next, pa_hat, ga_hat, pb_hat, gb_hat,
           e_own, e_prev, e_next, d_own, tap_own, tap_all, fg_part, c_recv, y_send, y_recv,
           x_send, x_recv, z_send, z_recv, final,
           in_sem, p_ssem, p_rsem, g_ssem, g_rsem, tz_ssem, tz_rsem, tx_ssem, tx_rsem,
           ty_ssem, ty_rsem, tc_ssem, tc_rsem, c_ssem, c_rsem, y_ssem, y_rsem,
           x_ssem, x_rsem, z_ssem, z_rsem, f_ssem, f_rsem):
    dp, ctx = lax.axis_index("dp"), lax.axis_index("ctx")
    DP, CTX, X, Y, Z = lay.dp, lay.ctx, lay.xs, lay.ys, lay.zs
    NC, HALF, GC, CH = lay.chunks, lay.half, lay.group, lay.chunk
    y, core = lax.div(dp, 2), lax.rem(dp, 2)
    x, z = lax.div(ctx, Z), lax.rem(ctx, Z)
    me = dp * CTX + ctx
    after, before = lax.rem(me + 1, DP * CTX), lax.rem(me + DP * CTX - 1, DP * CTX)
    place = lambda flat: (lax.div(flat, CTX), lax.rem(flat, CTX))
    nxt, prv = place(after), place(before)
    z_peer = lambda r: (dp, x * Z + lax.rem(z + r, Z))
    x_peer = lambda r: (dp, lax.rem(x + r, X) * Z + z)
    y_peer = lambda r: (2 * lax.rem(y + r, Y) + core, ctx)
    d_peer = lambda r: (lax.rem(dp + r, DP), ctx)
    partner = (2 * y + 1 - core, ctx)
    slot = core * Y + y

    barrier = pltpu.get_barrier_semaphore()
    peers = [nxt, prv] + [z_peer(r) for r in range(1, Z)]
    peers += [x_peer(r) for r in range(1, X)] + [d_peer(r) for r in range(1, DP)]
    for peer in peers:
        pl.semaphore_signal(barrier, inc=1, device_id=peer, device_id_type=MESH)

    def load(which, n):
        hbm, ref = ((q_hbm, q), (k_hbm, k), (v_hbm, v), (o_hbm, o))[which]
        return pltpu.make_async_copy(
            hbm.at[:, pl.ds(pl.multiple_of(n * CH, CH), CH)], ref.at[n], in_sem.at[which, n]
        )

    def start_loads(j, carry):
        for which, n in ((1, j), (2, j), (0, j + HALF), (3, j + HALF),
                         (1, j + HALF), (2, j + HALF), (0, j), (3, j)):
            load(which, n).start()
        return carry

    lax.fori_loop(0, HALF, start_loads, 0)

    turned = taps[...].T.astype(BF16)
    tap_own[...] = turned.reshape(DP, lay.rows, lay.lanes)
    tap_all[slot, ctx] = tap_own[slot]

    above, below = jnp.maximum(me - 1, 0), jnp.minimum(me + 1, DP * CTX - 1)
    own = docs[pl.ds(me, 1), :]
    first, last = own[:, :1], own[:, FL - 1 :]
    moved = (own != first).astype(F32)
    split = (first != last).astype(F32)
    keep_prev = (docs[pl.ds(above, 1), :] == first).astype(F32) * (me > 0).astype(F32)
    keep_next = (docs[pl.ds(below, 1), :] == last).astype(F32) * (me < DP * CTX - 1).astype(F32)
    twice = lambda row: jnp.concatenate([row, row], 1)
    t0, t1, t2 = (fwd_tab[i].astype(F32) for i in range(3))
    m = twice(moved)
    e_own[...] = (t0 * (1.0 - m) + t1 * m).astype(BF16)
    e_prev[...] = (-t2 * twice(keep_prev)).astype(BF16)
    e_next[...] = ((t1 * (1.0 - split) + t2 * split) * twice(keep_next)).astype(BF16)
    square = jnp.broadcast_to(moved, (FL, FL)).T
    wide = jnp.concatenate([square] * (2 * N // FL), 1)
    for half in range(2):
        rows = pl.ds(half * FL, FL)
        d0, d1 = inv_tab[0, rows, :].astype(F32), inv_tab[1, rows, :].astype(F32)
        d_own[rows, :] = (d0 * (1.0 - wide) + d1 * wide).astype(BF16)

    def tap_z(r):
        here = tap_all.at[slot, ctx]
        return remote(here, here, tz_ssem.at[r - 1], tz_rsem.at[r - 1], z_peer(r))

    def tap_x(r):
        here = tap_all.at[slot, pl.ds(x * Z, Z)]
        return remote(here, here, tx_ssem.at[r - 1], tx_rsem.at[r - 1], x_peer(r))

    def tap_y(r):
        here = tap_all.at[slot]
        return remote(here, here, ty_ssem.at[r - 1], ty_rsem.at[r - 1], y_peer(r))

    def tap_c():
        here = tap_all.at[pl.ds(core * Y, Y)]
        return remote(here, here, tc_ssem, tc_rsem, partner)

    def halo_p(n):
        return remote(p.at[n], p_prev.at[n], p_ssem.at[n], p_rsem.at[n], nxt)

    def halo_g(n):
        return remote(g.at[n], g_next.at[n], g_ssem.at[n], g_rsem.at[n], prv)

    def pair(n):
        return remote(fg_part.at[n, 1 - core], c_recv.at[n], c_ssem.at[n], c_rsem.at[n], partner)

    def part_y(r, group):
        chunks = pl.ds(group * GC, GC)
        return remote(y_send.at[lax.rem(y + r, Y), chunks], y_recv.at[r - 1, chunks],
                      y_ssem.at[r - 1, group], y_rsem.at[r - 1, group], y_peer(r))

    def part_x(r):
        return remote(x_send.at[pl.ds(lax.rem(x + r, X) * GC, GC)], x_recv.at[r - 1],
                      x_ssem.at[r - 1], x_rsem.at[r - 1], x_peer(r))

    def part_z(r):
        return remote(z_send.at[lax.rem(z + r, Z)], z_recv.at[r - 1],
                      z_ssem.at[r - 1], z_rsem.at[r - 1], z_peer(r))

    def part_f(r):
        here = final.at[slot]
        return remote(here, here, f_ssem.at[r - 1], f_rsem.at[r - 1], d_peer(r))

    def produce(j):
        for n in (j, j + HALF):
            load(1, n).wait()
            load(2, n).wait()
            p[n] = (k[n].astype(F32) * v[n].astype(F32)).astype(BF16)
            load(0, n).wait()
            load(3, n).wait()
            g[n] = (q[n].astype(F32) * o[n].astype(F32)).astype(BF16)

    def send(n):
        halo_p(n).start()
        halo_g(lax.rem(n + HALF, NC)).start()

    def produce_and_send(j, carry):
        produce(j)
        send(j)
        return carry

    produce(0)
    pl.semaphore_wait(barrier, len(peers))
    for r in range(1, Z):
        tap_z(r).start()
    send(0)
    lax.fori_loop(1, lay.ahead, produce_and_send, 0)

    def absorb(n):
        pair(n).wait_recv()
        y_send[:, n] = (fg_part[n, core] + c_recv[n]).reshape(Y, lay.rows, CH)

    def send_groups(gi):
        for group in (gi, gi + X // 2):
            for r in range(1, Y):
                part_y(r, group).start()

    def relay_x():
        for r in range(1, Z):
            tap_z(r).wait_recv()
        for r in range(1, X):
            tap_x(r).start()

    def relay_y():
        for r in range(1, X):
            tap_x(r).wait_recv()
        for r in range(1, Y):
            tap_y(r).start()

    def relay_c():
        for r in range(1, Y):
            tap_y(r).wait_recv()
        tap_c().start()

    def sum_y():
        for r in range(1, Y):
            for group in range(X):
                part_y(r, group).wait_recv()
        total = y_send[y]
        for r in range(1, Y):
            total = total + y_recv[r - 1]
        x_send[...] = total
        for r in range(1, X):
            part_x(r).start()

    def sum_x():
        for r in range(1, X):
            part_x(r).wait_recv()
        total = x_send[pl.ds(x * GC, GC)]
        for r in range(1, X):
            total = total + x_recv[r - 1]
        per = CH // lay.lanes
        for i in range(Z):
            lane = (i % per) * lay.lanes
            z_send[i] = total[i // per, :, lane : lane + lay.lanes]
        for r in range(1, Z):
            part_z(r).start()

    def sum_z():
        for r in range(1, Z):
            part_z(r).wait_recv()
        total = z_send[z]
        for r in range(1, Z):
            total = total + z_recv[r - 1]
        final[slot] = total
        for r in range(1, DP):
            part_f(r).start()

    def scheduled(j, events):
        for step, event in events:
            if step < HALF:
                pl.when(j == step)(event)

    early = ((1, relay_x), (3, relay_y), (6, relay_c))
    late = ((2, sum_y), (4, sum_x), (6, sum_z))

    def first_half(j, carry):
        @pl.when(j + lay.ahead < HALF)
        def _():
            produce(j + lay.ahead)

        @pl.when(j + lay.ahead < NC)
        def _():
            send(j + lay.ahead)

        scheduled(j, early)
        a, b = j, j + HALF
        ga = forward(e_own[...], g[a])
        pb = forward(e_own[...], p[b])
        ga_hat[j] = ga
        pb_hat[j] = pb
        pa = forward(e_own[...], p[a])
        halo_p(a).wait_recv()
        pa = pa + forward(e_prev[...], p_prev[a])
        pa_hat[j] = pa
        fg_part[a] = inverse(inv_tab[0], *correlate(pa, ga)).reshape(2, FL // 2, CH)
        pair(a).start()
        gb = forward(e_own[...], g[b])
        halo_g(b).wait_recv()
        gb = gb + forward(e_next[...], g_next[b])
        gb_hat[j] = gb
        fg_part[b] = inverse(inv_tab[0], *correlate(pb, gb)).reshape(2, FL // 2, CH)
        pair(b).start()

        @pl.when(j > 0)
        def _():
            absorb(j - 1)
            absorb(j - 1 + HALF)

        @pl.when((j > 0) & (lax.rem(j, GC) == 0))
        def _():
            send_groups(lax.div(j, GC) - 1)

        return carry

    lax.fori_loop(0, HALF, first_half, 0)
    for step, event in early:
        if step >= HALF:
            event()
    absorb(HALF - 1)
    absorb(NC - 1)
    send_groups(HALF // GC - 1)
    tap_c().wait_recv()

    def taps_of(n):
        per = CH // lay.lanes
        return jnp.concatenate(
            [tap_all[:, n * per + i].reshape(FL, lay.lanes) for i in range(per)], 1
        )

    def rounded(value):
        return (value * (1.0 / BINS)).astype(BF16).astype(F32)

    def write_query(n, mixed):
        cols = pl.ds(pl.multiple_of(n * CH, CH), CH)
        qg_ref[:, cols] = (o[n].astype(F32) * mixed).astype(BF16)

    def write_kv(n, back):
        cols = pl.ds(pl.multiple_of(n * CH, CH), CH)
        kg_ref[:, cols] = (back * v[n].astype(F32)).astype(BF16)
        vg_ref[:, cols] = (back * k[n].astype(F32)).astype(BF16)

    def second_half(j, carry):
        @pl.when(j + HALF + lay.ahead < NC)
        def _():
            send(j + HALF + lay.ahead)

        scheduled(j, late)
        a, b = j, j + HALF
        ha = forward(fwd_tab[0], taps_of(a))
        write_query(a, rounded(inverse(d_own[...], *convolve(ha, pa_hat[j]))))
        hb = forward(fwd_tab[0], taps_of(b))
        write_kv(b, rounded(inverse(d_own[...], *correlate(hb, gb_hat[j]))))
        halo_g(a).wait_recv()
        ga = ga_hat[j] + forward(e_next[...], g_next[a])
        write_kv(a, rounded(inverse(d_own[...], *correlate(ha, ga))))
        halo_p(b).wait_recv()
        pb = pb_hat[j] + forward(e_prev[...], p_prev[b])
        write_query(b, rounded(inverse(d_own[...], *convolve(hb, pb))))
        return carry

    lax.fori_loop(0, HALF, second_half, 0)
    for step, event in late:
        if step >= HALF:
            event()
    for r in range(1, DP):
        part_f(r).wait_recv()
    fg_ref[...] = final[...].reshape(FL, lay.lanes).T * (scale / BINS)

    def drain(n, carry):
        halo_p(n).wait_send()
        halo_g(n).wait_send()
        pair(n).wait_send()
        return carry

    lax.fori_loop(0, NC, drain, 0)
    for r in range(1, Z):
        tap_z(r).wait_send()
        part_z(r).wait_send()
    for r in range(1, X):
        tap_x(r).wait_send()
        part_x(r).wait_send()
    for r in range(1, Y):
        tap_y(r).wait_send()
        for group in range(X):
            part_y(r, group).wait_send()
    for r in range(1, DP):
        part_f(r).wait_send()
    tap_c().wait_send()


def shards(query_act, key_act, value_act, out_grad, filter_taps, doc_ids):
    rows, chans = key_act.shape
    lay = Layout(lax.axis_size("dp"), lax.axis_size("ctx"), chans)
    scale = 1.0 / math.sqrt(doc_ids.shape[0])
    fwd_tab, inv_tab = tables()
    acts = jax.ShapeDtypeStruct((rows, chans), BF16)
    any_spec, vmem = pl.BlockSpec(memory_space=pl.ANY), pl.BlockSpec(memory_space=pltpu.VMEM)
    NC, CH, GC, DP, X, Y, Z = (
        lay.chunks, lay.chunk, lay.group, lay.dp, lay.xs, lay.ys, lay.zs
    )
    block = pltpu.VMEM((NC, FL, CH), BF16)
    spectra = pltpu.VMEM((lay.half, N, CH), F32)
    mat = pltpu.VMEM((N, 2 * FL), BF16)
    dma = pltpu.SemaphoreType.DMA
    return pl.pallas_call(
        functools.partial(kernel, lay, scale),
        in_specs=[any_spec] * 4 + [vmem] * 4,
        out_specs=[vmem] * 4,
        out_shape=[acts, acts, acts, jax.ShapeDtypeStruct(filter_taps.shape, F32)],
        scratch_shapes=[block] * 8 + [spectra] * 4 + [
            mat, mat, mat,
            pltpu.VMEM((2 * FL, 2 * N), BF16),
            pltpu.VMEM((DP, lay.rows, lay.lanes), BF16),
            pltpu.VMEM((DP, lay.ctx, lay.rows, lay.lanes), BF16),
            pltpu.VMEM((NC, 2, FL // 2, CH), F32),
            pltpu.VMEM((NC, FL // 2, CH), F32),
            pltpu.VMEM((Y, NC, lay.rows, CH), F32),
            pltpu.VMEM((Y - 1, NC, lay.rows, CH), F32),
            pltpu.VMEM((NC, lay.rows, CH), F32),
            pltpu.VMEM((X - 1, GC, lay.rows, CH), F32),
            pltpu.VMEM((Z, lay.rows, lay.lanes), F32),
            pltpu.VMEM((Z - 1, lay.rows, lay.lanes), F32),
            pltpu.VMEM((DP, lay.rows, lay.lanes), F32),
            dma((4, NC)), dma((NC,)), dma((NC,)), dma((NC,)), dma((NC,)),
            dma((Z - 1,)), dma((Z - 1,)), dma((X - 1,)), dma((X - 1,)),
            dma((Y - 1,)), dma((Y - 1,)), dma, dma, dma((NC,)), dma((NC,)),
            dma((Y - 1, X)), dma((Y - 1, X)), dma((X - 1,)), dma((X - 1,)),
            dma((Z - 1,)), dma((Z - 1,)), dma((DP - 1,)), dma((DP - 1,)),
        ],
        compiler_params=pltpu.CompilerParams(
            collective_id=0, has_side_effects=True, vmem_limit_bytes=60 * 2**20
        ),
        name="mixer",
    )(query_act, key_act, value_act, out_grad, filter_taps,
      doc_ids.reshape(-1, FL), jnp.asarray(fwd_tab), jnp.asarray(inv_tab))


def solution(mesh):
    act = P(("dp", "ctx"), None)
    return jax.shard_map(
        shards,
        mesh=mesh,
        in_specs=(act, act, act, act, P("ctx", None), P()),
        out_specs=(act, act, act, P("ctx", None)),
        check_vma=False,
    )
```

```python
import functools
import math

import jax
import jax.numpy as jnp
import numpy as np
import ml_dtypes
from jax import lax
from jax.experimental import pallas as pl
from jax.experimental.pallas import tpu as pltpu
from jax.sharding import PartitionSpec as P

FL = 128
BINS = 192
N = 2 * BINS
CHUNK = 256
F32 = jnp.float32
BF16 = jnp.bfloat16


def tables():
    k = np.arange(BINS)[:, None]
    fwd, inv = [], []
    for block in range(3):
        u = np.arange(FL)[None, :] + FL * block
        angle = np.pi * ((2 * k + 1) * u % (2 * N)) / N
        full = np.concatenate([np.cos(angle), np.sin(angle)], 0)
        high = full.astype(ml_dtypes.bfloat16)
        low = (full - high.astype(np.float64)).astype(ml_dtypes.bfloat16)
        fwd.append(np.concatenate([high, low], 1))
        zero = np.zeros_like(low.T)
        inv.append(
            np.concatenate(
                [np.concatenate([high.T, high.T], 1), np.concatenate([low.T, zero], 1)], 0
            )
        )
    return np.stack(fwd), np.stack(inv[:2])


def forward(matrix, block):
    return jnp.dot(
        matrix, jnp.concatenate([block, block], 0), preferred_element_type=F32
    )


def inverse(matrix, cosines, sines):
    spectrum = jnp.concatenate([cosines, sines], 0)
    high = spectrum.astype(BF16)
    low = (spectrum - high.astype(F32)).astype(BF16)
    both = jnp.dot(matrix, jnp.concatenate([high, low], 0), preferred_element_type=F32)
    return both[:FL] + both[FL:]


def convolve(a, b):
    ca, sa, cb, sb = a[:BINS], a[BINS:], b[:BINS], b[BINS:]
    return ca * cb - sa * sb, ca * sb + sa * cb


def correlate(a, b):
    ca, sa, cb, sb = a[:BINS], a[BINS:], b[:BINS], b[BINS:]
    return ca * cb + sa * sb, ca * sb - sa * cb

MESH = pl.DeviceIdType.MESH


class Layout:
    def __init__(self, dp, ctx, chans, chunk=CHUNK):
        self.dp, self.ctx, self.cores, self.ys = dp, ctx, 2, dp // 2
        self.zs = 8 if ctx == 32 else ctx // 2
        self.xs = ctx // self.zs
        self.chans, self.chunk = chans, chunk
        self.chunks = chans // chunk
        self.half = self.chunks // 2
        self.group = self.chunks // self.xs
        self.rows = FL // dp
        self.lanes = chans // ctx


def remote(src, dst, send, recv, device):
    return pltpu.make_async_remote_copy(
        src_ref=src, dst_ref=dst, send_sem=send, recv_sem=recv, device_id=device,
        device_id_type=MESH,
    )


def kernel(lay, q_hbm, k_hbm, v_hbm, o_hbm, taps, docs, fwd_tab, inv_tab,
           mixed_ref, back_ref, fg_ref,
           q, k, v, o, p, g, p_prev, g_next, pa_hat, ga_hat, pb_hat, gb_hat,
           e_own, e_prev, e_next, d_own, tap_own, tap_all, fg_part, c_recv, y_send, y_recv,
           x_send, x_recv, z_send, z_recv, final,
           in_sem, p_ssem, p_rsem, g_ssem, g_rsem, tz_ssem, tz_rsem, tx_ssem, tx_rsem,
           ty_ssem, ty_rsem, tc_ssem, tc_rsem, c_ssem, c_rsem, y_ssem, y_rsem,
           x_ssem, x_rsem, z_ssem, z_rsem, f_ssem, f_rsem):
    dp, ctx = lax.axis_index("dp"), lax.axis_index("ctx")
    DP, CTX, X, Y, Z = lay.dp, lay.ctx, lay.xs, lay.ys, lay.zs
    NC, HALF, GC, CH = lay.chunks, lay.half, lay.group, lay.chunk
    y, core = lax.div(dp, 2), lax.rem(dp, 2)
    x, z = lax.div(ctx, Z), lax.rem(ctx, Z)
    me = dp * CTX + ctx
    after, before = lax.rem(me + 1, DP * CTX), lax.rem(me + DP * CTX - 1, DP * CTX)
    place = lambda flat: (lax.div(flat, CTX), lax.rem(flat, CTX))
    nxt, prv = place(after), place(before)
    z_peer = lambda r: (dp, x * Z + lax.rem(z + r, Z))
    x_peer = lambda r: (dp, lax.rem(x + r, X) * Z + z)
    y_peer = lambda r: (2 * lax.rem(y + r, Y) + core, ctx)
    d_peer = lambda r: (lax.rem(dp + r, DP), ctx)
    partner = (2 * y + 1 - core, ctx)
    slot = core * Y + y

    barrier = pltpu.get_barrier_semaphore()
    peers = [nxt, prv] + [z_peer(r) for r in range(1, Z)]
    peers += [x_peer(r) for r in range(1, X)] + [d_peer(r) for r in range(1, DP)]
    for peer in peers:
        pl.semaphore_signal(barrier, inc=1, device_id=peer, device_id_type=MESH)

    def load(which, n):
        hbm, ref = ((q_hbm, q), (k_hbm, k), (v_hbm, v), (o_hbm, o))[which]
        return pltpu.make_async_copy(
            hbm.at[:, pl.ds(pl.multiple_of(n * CH, CH), CH)], ref.at[n], in_sem.at[which, n]
        )

    def start_loads(j, carry):
        for which, n in ((1, j), (2, j), (0, j + HALF), (3, j + HALF),
                         (1, j + HALF), (2, j + HALF), (0, j), (3, j)):
            load(which, n).start()
        return carry

    lax.fori_loop(0, HALF, start_loads, 0)

    turned = taps[...].T.astype(BF16)
    tap_own[...] = turned.reshape(DP, lay.rows, lay.lanes)
    tap_all[slot, ctx] = tap_own[slot]

    above, below = jnp.maximum(me - 1, 0), jnp.minimum(me + 1, DP * CTX - 1)
    own = docs[pl.ds(me, 1), :]
    first, last = own[:, :1], own[:, FL - 1 :]
    moved = (own != first).astype(F32)
    split = (first != last).astype(F32)
    keep_prev = (docs[pl.ds(above, 1), :] == first).astype(F32) * (me > 0).astype(F32)
    keep_next = (docs[pl.ds(below, 1), :] == last).astype(F32) * (me < DP * CTX - 1).astype(F32)
    twice = lambda row: jnp.concatenate([row, row], 1)
    t0, t1, t2 = (fwd_tab[i].astype(F32) for i in range(3))
    m = twice(moved)
    e_own[...] = (t0 * (1.0 - m) + t1 * m).astype(BF16)
    e_prev[...] = (-t2 * twice(keep_prev)).astype(BF16)
    e_next[...] = ((t1 * (1.0 - split) + t2 * split) * twice(keep_next)).astype(BF16)
    square = jnp.broadcast_to(moved, (FL, FL)).T
    wide = jnp.concatenate([square] * (2 * N // FL), 1)
    for half in range(2):
        rows = pl.ds(half * FL, FL)
        d0, d1 = inv_tab[0, rows, :].astype(F32), inv_tab[1, rows, :].astype(F32)
        d_own[rows, :] = (d0 * (1.0 - wide) + d1 * wide).astype(BF16)

    def tap_z(r):
        here = tap_all.at[slot, ctx]
        return remote(here, here, tz_ssem.at[r - 1], tz_rsem.at[r - 1], z_peer(r))

    def tap_x(r):
        here = tap_all.at[slot, pl.ds(x * Z, Z)]
        return remote(here, here, tx_ssem.at[r - 1], tx_rsem.at[r - 1], x_peer(r))

    def tap_y(r):
        here = tap_all.at[slot]
        return remote(here, here, ty_ssem.at[r - 1], ty_rsem.at[r - 1], y_peer(r))

    def tap_c():
        here = tap_all.at[pl.ds(core * Y, Y)]
        return remote(here, here, tc_ssem, tc_rsem, partner)

    def halo_p(n):
        return remote(p.at[n], p_prev.at[n], p_ssem.at[n], p_rsem.at[n], nxt)

    def halo_g(n):
        return remote(g.at[n], g_next.at[n], g_ssem.at[n], g_rsem.at[n], prv)

    def pair(n):
        return remote(fg_part.at[n, 1 - core], c_recv.at[n], c_ssem.at[n], c_rsem.at[n], partner)

    def part_y(r, group):
        chunks = pl.ds(group * GC, GC)
        return remote(y_send.at[lax.rem(y + r, Y), chunks], y_recv.at[r - 1, chunks],
                      y_ssem.at[r - 1, group], y_rsem.at[r - 1, group], y_peer(r))

    def part_x(r):
        return remote(x_send.at[pl.ds(lax.rem(x + r, X) * GC, GC)], x_recv.at[r - 1],
                      x_ssem.at[r - 1], x_rsem.at[r - 1], x_peer(r))

    def part_z(r):
        return remote(z_send.at[lax.rem(z + r, Z)], z_recv.at[r - 1],
                      z_ssem.at[r - 1], z_rsem.at[r - 1], z_peer(r))

    def part_f(r):
        here = final.at[slot]
        return remote(here, here, f_ssem.at[r - 1], f_rsem.at[r - 1], d_peer(r))

    def produce(j):
        for n in (j, j + HALF):
            load(1, n).wait()
            load(2, n).wait()
            p[n] = (k[n].astype(F32) * v[n].astype(F32)).astype(BF16)
            load(0, n).wait()
            load(3, n).wait()
            g[n] = (q[n].astype(F32) * o[n].astype(F32)).astype(BF16)

    def send(n):
        halo_p(n).start()
        halo_g(lax.rem(n + HALF, NC)).start()

    def produce_and_send(j, carry):
        produce(j)
        send(j)
        return carry

    def send_rest(n, carry):
        send(n)
        return carry

    produce(0)
    pl.semaphore_wait(barrier, len(peers))
    for r in range(1, Z):
        tap_z(r).start()
    send(0)
    lax.fori_loop(1, HALF, produce_and_send, 0)
    lax.fori_loop(HALF, NC, send_rest, 0)

    def absorb(n):
        pair(n).wait_recv()
        y_send[:, n] = (fg_part[n, core] + c_recv[n]).astype(BF16)

    def send_groups(gi):
        for group in (gi, gi + X // 2):
            for r in range(1, Y):
                part_y(r, group).start()

    def relay_x():
        for r in range(1, Z):
            tap_z(r).wait_recv()
        for r in range(1, X):
            tap_x(r).start()

    def relay_y():
        for r in range(1, X):
            tap_x(r).wait_recv()
        for r in range(1, Y):
            tap_y(r).start()

    def relay_c():
        for r in range(1, Y):
            tap_y(r).wait_recv()
        tap_c().start()

    def sum_y():
        for r in range(1, Y):
            for group in range(X):
                part_y(r, group).wait_recv()
        total = fg_part[:, core, y] + c_recv[:, y]
        for r in range(1, Y):
            total = total + y_recv[r - 1].astype(F32)
        x_send[...] = total
        for r in range(1, X):
            part_x(r).start()

    def sum_x():
        for r in range(1, X):
            part_x(r).wait_recv()
        total = x_send[pl.ds(x * GC, GC)]
        for r in range(1, X):
            total = total + x_recv[r - 1]
        per = CH // lay.lanes
        for i in range(Z):
            lane = (i % per) * lay.lanes
            z_send[i] = total[i // per, :, lane : lane + lay.lanes]
        for r in range(1, Z):
            part_z(r).start()

    def sum_z():
        for r in range(1, Z):
            part_z(r).wait_recv()
        total = z_send[z]
        for r in range(1, Z):
            total = total + z_recv[r - 1]
        final[slot] = total
        for r in range(1, DP):
            part_f(r).start()

    def scheduled(j, events):
        for step, event in events:
            if step < HALF:
                pl.when(j == step)(event)

    early = ((2, relay_x), (5, relay_y), (HALF, relay_c))
    late = ((2, sum_y), (4, sum_x), (6, sum_z))

    def first_half(j, carry):
        scheduled(j, early)
        a, b = j, j + HALF
        ga = forward(e_own[...], g[a])
        pb = forward(e_own[...], p[b])
        ga_hat[j] = ga
        pb_hat[j] = pb
        pa = forward(e_own[...], p[a])
        halo_p(a).wait_recv()
        pa = pa + forward(e_prev[...], p_prev[a])
        pa_hat[j] = pa
        fg_part[a] = inverse(inv_tab[0], *correlate(pa, ga)).reshape(2, Y, lay.rows, CH)
        pair(a).start()
        gb = forward(e_own[...], g[b])
        halo_g(b).wait_recv()
        gb = gb + forward(e_next[...], g_next[b])
        gb_hat[j] = gb
        fg_part[b] = inverse(inv_tab[0], *correlate(pb, gb)).reshape(2, Y, lay.rows, CH)
        pair(b).start()

        @pl.when(j > 0)
        def _():
            absorb(j - 1)
            absorb(j - 1 + HALF)

        @pl.when((j > 0) & (lax.rem(j, GC) == 0))
        def _():
            send_groups(lax.div(j, GC) - 1)

        return carry

    lax.fori_loop(0, HALF, first_half, 0)
    for step, event in early:
        if step >= HALF:
            event()
    absorb(HALF - 1)
    absorb(NC - 1)
    send_groups(HALF // GC - 1)
    tap_c().wait_recv()

    def taps_of(n):
        per = CH // lay.lanes
        return jnp.concatenate(
            [tap_all[:, n * per + i].reshape(FL, lay.lanes) for i in range(per)], 1
        )

    def write(ref, n, value):
        cols = pl.ds(pl.multiple_of(n * CH, CH), CH)
        ref[:, cols] = (value * (1.0 / BINS)).astype(BF16)

    def second_half(j, carry):
        scheduled(j, late)
        a, b = j, j + HALF
        ha = forward(fwd_tab[0], taps_of(a))
        write(mixed_ref, a, inverse(d_own[...], *convolve(ha, pa_hat[j])))
        hb = forward(fwd_tab[0], taps_of(b))
        write(back_ref, b, inverse(d_own[...], *correlate(hb, gb_hat[j])))
        halo_g(a).wait_recv()
        ga = ga_hat[j] + forward(e_next[...], g_next[a])
        write(back_ref, a, inverse(d_own[...], *correlate(ha, ga)))
        halo_p(b).wait_recv()
        pb = pb_hat[j] + forward(e_prev[...], p_prev[b])
        write(mixed_ref, b, inverse(d_own[...], *convolve(hb, pb)))
        return carry

    lax.fori_loop(0, HALF, second_half, 0)
    for step, event in late:
        if step >= HALF:
            event()
    for r in range(1, DP):
        part_f(r).wait_recv()
    fg_ref[...] = final[...].reshape(FL, lay.lanes).T

    def drain(n, carry):
        halo_p(n).wait_send()
        halo_g(n).wait_send()
        pair(n).wait_send()
        return carry

    lax.fori_loop(0, NC, drain, 0)
    for r in range(1, Z):
        tap_z(r).wait_send()
        part_z(r).wait_send()
    for r in range(1, X):
        tap_x(r).wait_send()
        part_x(r).wait_send()
    for r in range(1, Y):
        tap_y(r).wait_send()
        for group in range(X):
            part_y(r, group).wait_send()
    for r in range(1, DP):
        part_f(r).wait_send()
    tap_c().wait_send()


def shards(query_act, key_act, value_act, out_grad, filter_taps, doc_ids):
    rows, chans = key_act.shape
    lay = Layout(lax.axis_size("dp"), lax.axis_size("ctx"), chans)
    scale = 1.0 / math.sqrt(doc_ids.shape[0])
    fwd_tab, inv_tab = tables()
    acts = jax.ShapeDtypeStruct((rows, chans), BF16)
    any_spec, vmem = pl.BlockSpec(memory_space=pl.ANY), pl.BlockSpec(memory_space=pltpu.VMEM)
    NC, CH, GC, DP, X, Y, Z = (
        lay.chunks, lay.chunk, lay.group, lay.dp, lay.xs, lay.ys, lay.zs
    )
    block = pltpu.VMEM((NC, FL, CH), BF16)
    spectra = pltpu.VMEM((lay.half, N, CH), F32)
    mat = pltpu.VMEM((N, 2 * FL), BF16)
    dma = pltpu.SemaphoreType.DMA
    mixed, back, filter_grad = pl.pallas_call(
        functools.partial(kernel, lay),
        in_specs=[any_spec] * 4 + [vmem] * 4,
        out_specs=[vmem] * 3,
        out_shape=[acts, acts, jax.ShapeDtypeStruct(filter_taps.shape, F32)],
        scratch_shapes=[block] * 8 + [spectra] * 4 + [
            mat, mat, mat,
            pltpu.VMEM((2 * FL, 2 * N), BF16),
            pltpu.VMEM((DP, lay.rows, lay.lanes), BF16),
            pltpu.VMEM((DP, lay.ctx, lay.rows, lay.lanes), BF16),
            pltpu.VMEM((NC, 2, Y, lay.rows, CH), F32),
            pltpu.VMEM((NC, Y, lay.rows, CH), F32),
            pltpu.VMEM((Y, NC, lay.rows, CH), BF16),
            pltpu.VMEM((Y - 1, NC, lay.rows, CH), BF16),
            pltpu.VMEM((NC, lay.rows, CH), F32),
            pltpu.VMEM((X - 1, GC, lay.rows, CH), F32),
            pltpu.VMEM((Z, lay.rows, lay.lanes), F32),
            pltpu.VMEM((Z - 1, lay.rows, lay.lanes), F32),
            pltpu.VMEM((DP, lay.rows, lay.lanes), F32),
            dma((4, NC)), dma((NC,)), dma((NC,)), dma((NC,)), dma((NC,)),
            dma((Z - 1,)), dma((Z - 1,)), dma((X - 1,)), dma((X - 1,)),
            dma((Y - 1,)), dma((Y - 1,)), dma, dma, dma((NC,)), dma((NC,)),
            dma((Y - 1, X)), dma((Y - 1, X)), dma((X - 1,)), dma((X - 1,)),
            dma((Z - 1,)), dma((Z - 1,)), dma((DP - 1,)), dma((DP - 1,)),
        ],
        compiler_params=pltpu.CompilerParams(
            collective_id=0, has_side_effects=True, vmem_limit_bytes=60 * 2**20
        ),
        name="mixer",
    )(query_act, key_act, value_act, out_grad, filter_taps,
      doc_ids.reshape(-1, FL), jnp.asarray(fwd_tab), jnp.asarray(inv_tab))
    mixed, back = mixed.astype(F32), back.astype(F32)
    query_grad = (out_grad.astype(F32) * mixed).astype(BF16)
    key_grad = (back * value_act.astype(F32)).astype(BF16)
    value_grad = (back * key_act.astype(F32)).astype(BF16)
    return query_grad, key_grad, value_grad, filter_grad * (scale / BINS)


def solution(mesh):
    act = P(("dp", "ctx"), None)
    return jax.shard_map(
        shards,
        mesh=mesh,
        in_specs=(act, act, act, act, P("ctx", None), P()),
        out_specs=(act, act, act, P("ctx", None)),
        check_vma=False,
    )
```

```python
import functools
import math

import jax
import jax.numpy as jnp
import numpy as np
import ml_dtypes
from jax import lax
from jax.experimental import pallas as pl
from jax.experimental.pallas import tpu as pltpu
from jax.sharding import PartitionSpec as P

FL = 128
BINS = 192
N = 2 * BINS
CHUNK = 256
F32 = jnp.float32
BF16 = jnp.bfloat16


def tables():
    k = np.arange(BINS)[:, None]
    fwd, inv = [], []
    for block in range(3):
        u = np.arange(FL)[None, :] + FL * block
        angle = np.pi * ((2 * k + 1) * u % (2 * N)) / N
        full = np.concatenate([np.cos(angle), np.sin(angle)], 0)
        high = full.astype(ml_dtypes.bfloat16)
        low = (full - high.astype(np.float64)).astype(ml_dtypes.bfloat16)
        fwd.append(np.concatenate([high, low], 1))
        zero = np.zeros_like(low.T)
        inv.append(
            np.concatenate(
                [np.concatenate([high.T, high.T], 1), np.concatenate([low.T, zero], 1)], 0
            )
        )
    return np.stack(fwd), np.stack(inv[:2])


def forward(matrix, block):
    return jnp.dot(
        matrix, jnp.concatenate([block, block], 0), preferred_element_type=F32
    )


def inverse(matrix, cosines, sines):
    spectrum = jnp.concatenate([cosines, sines], 0)
    high = spectrum.astype(BF16)
    low = (spectrum - high.astype(F32)).astype(BF16)
    both = jnp.dot(matrix, jnp.concatenate([high, low], 0), preferred_element_type=F32)
    return both[:FL] + both[FL:]


def convolve(a, b):
    ca, sa, cb, sb = a[:BINS], a[BINS:], b[:BINS], b[BINS:]
    return ca * cb - sa * sb, ca * sb + sa * cb


def correlate(a, b):
    ca, sa, cb, sb = a[:BINS], a[BINS:], b[:BINS], b[BINS:]
    return ca * cb + sa * sb, ca * sb - sa * cb

MESH = pl.DeviceIdType.MESH


class Layout:
    def __init__(self, dp, ctx, chans, chunk=CHUNK):
        self.dp, self.ctx, self.cores, self.ys = dp, ctx, 2, dp // 2
        self.chans, self.chunk = chans, chunk
        self.chunks = chans // chunk
        self.half = self.chunks // 2
        self.batch = max(1, self.half // 4)
        self.rows = FL // dp
        self.lanes = chans // ctx


def remote(src, dst, send, recv, device):
    return pltpu.make_async_remote_copy(
        src_ref=src, dst_ref=dst, send_sem=send, recv_sem=recv, device_id=device,
        device_id_type=MESH,
    )


def kernel(lay, scale, q_hbm, k_hbm, v_hbm, o_hbm, taps, docs, fwd_tab, inv_tab,
           mixed_ref, back_ref, fg_ref,
           q, k, v, o, p, g, p_prev, g_next, pa_hat, ga_hat, pb_hat, gb_hat,
           e_own, e_prev, e_next, d_own, tap_own, tap_all, fg_part, c_recv, y_send, y_recv,
           x_own, x_send, x_recv, final,
           in_sem, p_ssem, p_rsem, g_ssem, g_rsem, tx_ssem, tx_rsem,
           ty_ssem, ty_rsem, tc_ssem, tc_rsem, c_ssem, c_rsem, y_ssem, y_rsem,
           x_ssem, x_rsem, f_ssem, f_rsem):
    dp, ctx = lax.axis_index("dp"), lax.axis_index("ctx")
    DP, CTX, Y = lay.dp, lay.ctx, lay.ys
    NC, HALF, YB, CH = lay.chunks, lay.half, lay.batch, lay.chunk
    y, core = lax.div(dp, 2), lax.rem(dp, 2)
    me = dp * CTX + ctx
    after, before = lax.rem(me + 1, DP * CTX), lax.rem(me + DP * CTX - 1, DP * CTX)
    place = lambda flat: (lax.div(flat, CTX), lax.rem(flat, CTX))
    nxt, prv = place(after), place(before)
    c_peer = lambda r: (dp, lax.rem(ctx + r, CTX))
    y_peer = lambda r: (2 * lax.rem(y + r, Y) + core, ctx)
    d_peer = lambda r: (lax.rem(dp + r, DP), ctx)
    partner = (2 * y + 1 - core, ctx)
    slot = core * Y + y

    barrier = pltpu.get_barrier_semaphore()
    peers = [nxt, prv] + [d_peer(r) for r in range(1, DP)]
    for peer in peers:
        pl.semaphore_signal(barrier, inc=1, device_id=peer, device_id_type=MESH)

    def greet(r, carry):
        pl.semaphore_signal(barrier, inc=1, device_id=c_peer(r), device_id_type=MESH)
        return carry

    lax.fori_loop(1, CTX, greet, 0)

    def load(which, n):
        hbm, ref = ((q_hbm, q), (k_hbm, k), (v_hbm, v), (o_hbm, o))[which]
        return pltpu.make_async_copy(
            hbm.at[:, pl.ds(pl.multiple_of(n * CH, CH), CH)], ref.at[n], in_sem.at[which, n]
        )

    def start_loads(j, carry):
        for which, n in ((1, j), (2, j), (0, j + HALF), (3, j + HALF),
                         (1, j + HALF), (2, j + HALF), (0, j), (3, j)):
            load(which, n).start()
        return carry

    lax.fori_loop(0, HALF, start_loads, 0)

    turned = taps[...].T.astype(BF16)
    tap_own[...] = turned.reshape(DP, lay.rows, lay.lanes)
    tap_all[slot, ctx] = tap_own[slot]

    above, below = jnp.maximum(me - 1, 0), jnp.minimum(me + 1, DP * CTX - 1)
    own = docs[pl.ds(me, 1), :]
    first, last = own[:, :1], own[:, FL - 1 :]
    moved = (own != first).astype(F32)
    split = (first != last).astype(F32)
    keep_prev = (docs[pl.ds(above, 1), :] == first).astype(F32) * (me > 0).astype(F32)
    keep_next = (docs[pl.ds(below, 1), :] == last).astype(F32) * (me < DP * CTX - 1).astype(F32)
    twice = lambda row: jnp.concatenate([row, row], 1)
    t0, t1, t2 = (fwd_tab[i].astype(F32) for i in range(3))
    m = twice(moved)
    e_own[...] = (t0 * (1.0 - m) + t1 * m).astype(BF16)
    e_prev[...] = (-t2 * twice(keep_prev)).astype(BF16)
    e_next[...] = ((t1 * (1.0 - split) + t2 * split) * twice(keep_next)).astype(BF16)
    square = jnp.broadcast_to(moved, (FL, FL)).T
    wide = jnp.concatenate([square] * (2 * N // FL), 1)
    for half in range(2):
        rows = pl.ds(half * FL, FL)
        d0, d1 = inv_tab[0, rows, :].astype(F32), inv_tab[1, rows, :].astype(F32)
        d_own[rows, :] = (d0 * (1.0 - wide) + d1 * wide).astype(BF16)

    def tap_ctx(r):
        here = tap_all.at[slot, ctx]
        return remote(here, here, tx_ssem.at[r - 1], tx_rsem.at[r - 1], c_peer(r))

    def tap_y(r):
        here = tap_all.at[slot]
        return remote(here, here, ty_ssem.at[r - 1], ty_rsem.at[r - 1], y_peer(r))

    def tap_c():
        here = tap_all.at[pl.ds(core * Y, Y)]
        return remote(here, here, tc_ssem, tc_rsem, partner)

    def halo_p(n):
        return remote(p.at[n], p_prev.at[n], p_ssem.at[n], p_rsem.at[n], nxt)

    def halo_g(n):
        return remote(g.at[n], g_next.at[n], g_ssem.at[n], g_rsem.at[n], prv)

    def pair(n):
        return remote(fg_part.at[n, 1 - core], c_recv.at[n], c_ssem.at[n], c_rsem.at[n], partner)

    def part_y(r, group):
        chunks = pl.ds(group * YB, YB)
        return remote(y_send.at[lax.rem(y + r, Y), chunks], y_recv.at[r - 1, chunks],
                      y_ssem.at[r - 1, group], y_rsem.at[r - 1, group], y_peer(r))

    def part_ctx(r):
        return remote(x_send.at[lax.rem(ctx + r, CTX)], x_recv.at[r - 1],
                      x_ssem.at[r - 1], x_rsem.at[r - 1], c_peer(r))

    def each_peer(action):
        def body(r, carry):
            action(r)
            return carry

        lax.fori_loop(1, CTX, body, 0)

    def part_f(r):
        here = final.at[slot]
        return remote(here, here, f_ssem.at[r - 1], f_rsem.at[r - 1], d_peer(r))

    def produce(j):
        for n in (j, j + HALF):
            load(1, n).wait()
            load(2, n).wait()
            p[n] = (k[n].astype(F32) * v[n].astype(F32)).astype(BF16)
            load(0, n).wait()
            load(3, n).wait()
            g[n] = (q[n].astype(F32) * o[n].astype(F32)).astype(BF16)

    def send(n):
        halo_p(n).start()
        halo_g(lax.rem(n + HALF, NC)).start()

    def produce_and_send(j, carry):
        produce(j)
        send(j)
        return carry

    def send_rest(n, carry):
        send(n)
        return carry

    produce(0)
    pl.semaphore_wait(barrier, len(peers) + CTX - 1)
    each_peer(lambda r: tap_ctx(r).start())
    send(0)
    lax.fori_loop(1, HALF, produce_and_send, 0)
    lax.fori_loop(HALF, NC, send_rest, 0)

    def absorb(n):
        pair(n).wait_recv()
        y_send[:, n] = (fg_part[n, core] + c_recv[n]).astype(BF16)

    def send_groups(gi):
        for group in (gi, gi + HALF // YB):
            for r in range(1, Y):
                part_y(r, group).start()

    def relay_y():
        each_peer(lambda r: tap_ctx(r).wait_recv())
        for r in range(1, Y):
            tap_y(r).start()

    def relay_c():
        for r in range(1, Y):
            tap_y(r).wait_recv()
        tap_c().start()

    def sum_y():
        for r in range(1, Y):
            for group in range(NC // YB):
                part_y(r, group).wait_recv()
        total = fg_part[:, core, y] + c_recv[:, y]
        for r in range(1, Y):
            total = total + y_recv[r - 1].astype(F32)
        per = CH // lay.lanes
        for i in range(CTX):
            lane = (i % per) * lay.lanes
            piece = total[i // per, :, lane : lane + lay.lanes]
            x_own[i] = piece
            x_send[i] = piece.astype(BF16)
        each_peer(lambda r: part_ctx(r).start())

    def sum_ctx():
        each_peer(lambda r: part_ctx(r).wait_recv())
        final[slot] = x_own[ctx] + jnp.sum(x_recv[...].astype(F32), axis=0)
        for r in range(1, DP):
            part_f(r).start()

    def scheduled(j, events):
        for step, event in events:
            if step < HALF:
                pl.when(j == step)(event)

    early = ((4, relay_y), (HALF, relay_c))
    late = ((4, sum_y), (HALF, sum_ctx))

    def first_half(j, carry):
        scheduled(j, early)
        a, b = j, j + HALF
        ga = forward(e_own[...], g[a])
        pb = forward(e_own[...], p[b])
        ga_hat[j] = ga
        pb_hat[j] = pb
        pa = forward(e_own[...], p[a])
        halo_p(a).wait_recv()
        pa = pa + forward(e_prev[...], p_prev[a])
        pa_hat[j] = pa
        fg_part[a] = inverse(inv_tab[0], *correlate(pa, ga)).reshape(2, Y, lay.rows, CH)
        pair(a).start()
        gb = forward(e_own[...], g[b])
        halo_g(b).wait_recv()
        gb = gb + forward(e_next[...], g_next[b])
        gb_hat[j] = gb
        fg_part[b] = inverse(inv_tab[0], *correlate(pb, gb)).reshape(2, Y, lay.rows, CH)
        pair(b).start()

        @pl.when(j > 0)
        def _():
            absorb(j - 1)
            absorb(j - 1 + HALF)

        @pl.when((j > 0) & (lax.rem(j, YB) == 0))
        def _():
            send_groups(lax.div(j, YB) - 1)

        return carry

    lax.fori_loop(0, HALF, first_half, 0)
    for step, event in early:
        if step >= HALF:
            event()
    absorb(HALF - 1)
    absorb(NC - 1)
    send_groups(HALF // YB - 1)
    tap_c().wait_recv()

    def taps_of(n):
        per = CH // lay.lanes
        return jnp.concatenate(
            [tap_all[:, n * per + i].reshape(FL, lay.lanes) for i in range(per)], 1
        )

    def write(ref, n, value):
        cols = pl.ds(pl.multiple_of(n * CH, CH), CH)
        ref[:, cols] = (value * (1.0 / BINS)).astype(BF16)

    def second_half(j, carry):
        scheduled(j, late)
        a, b = j, j + HALF
        ha = forward(fwd_tab[0], taps_of(a))
        write(mixed_ref, a, inverse(d_own[...], *convolve(ha, pa_hat[j])))
        hb = forward(fwd_tab[0], taps_of(b))
        write(back_ref, b, inverse(d_own[...], *correlate(hb, gb_hat[j])))
        halo_g(a).wait_recv()
        ga = ga_hat[j] + forward(e_next[...], g_next[a])
        write(back_ref, a, inverse(d_own[...], *correlate(ha, ga)))
        halo_p(b).wait_recv()
        pb = pb_hat[j] + forward(e_prev[...], p_prev[b])
        write(mixed_ref, b, inverse(d_own[...], *convolve(hb, pb)))
        return carry

    lax.fori_loop(0, HALF, second_half, 0)
    for step, event in late:
        if step >= HALF:
            event()
    for r in range(1, DP):
        part_f(r).wait_recv()
    fg_ref[...] = final[...].reshape(FL, lay.lanes).T * (scale / BINS)

    def drain(n, carry):
        halo_p(n).wait_send()
        halo_g(n).wait_send()
        pair(n).wait_send()
        return carry

    lax.fori_loop(0, NC, drain, 0)
    each_peer(lambda r: tap_ctx(r).wait_send())
    each_peer(lambda r: part_ctx(r).wait_send())
    for r in range(1, Y):
        tap_y(r).wait_send()
        for group in range(NC // YB):
            part_y(r, group).wait_send()
    for r in range(1, DP):
        part_f(r).wait_send()
    tap_c().wait_send()


def shards(query_act, key_act, value_act, out_grad, filter_taps, doc_ids):
    rows, chans = key_act.shape
    lay = Layout(lax.axis_size("dp"), lax.axis_size("ctx"), chans)
    scale = 1.0 / math.sqrt(doc_ids.shape[0])
    fwd_tab, inv_tab = tables()
    acts = jax.ShapeDtypeStruct((rows, chans), BF16)
    any_spec, vmem = pl.BlockSpec(memory_space=pl.ANY), pl.BlockSpec(memory_space=pltpu.VMEM)
    NC, CH, CTX, DP, Y = lay.chunks, lay.chunk, lay.ctx, lay.dp, lay.ys
    block = pltpu.VMEM((NC, FL, CH), BF16)
    spectra = pltpu.VMEM((lay.half, N, CH), F32)
    mat = pltpu.VMEM((N, 2 * FL), BF16)
    dma = pltpu.SemaphoreType.DMA
    mixed, back, filter_grad = pl.pallas_call(
        functools.partial(kernel, lay, scale),
        in_specs=[any_spec] * 4 + [vmem] * 4,
        out_specs=[vmem] * 3,
        out_shape=[acts, acts, jax.ShapeDtypeStruct(filter_taps.shape, F32)],
        scratch_shapes=[block] * 8 + [spectra] * 4 + [
            mat, mat, mat,
            pltpu.VMEM((2 * FL, 2 * N), BF16),
            pltpu.VMEM((DP, lay.rows, lay.lanes), BF16),
            pltpu.VMEM((DP, CTX, lay.rows, lay.lanes), BF16),
            pltpu.VMEM((NC, 2, Y, lay.rows, CH), F32),
            pltpu.VMEM((NC, Y, lay.rows, CH), F32),
            pltpu.VMEM((Y, NC, lay.rows, CH), BF16),
            pltpu.VMEM((Y - 1, NC, lay.rows, CH), BF16),
            pltpu.VMEM((CTX, lay.rows, lay.lanes), F32),
            pltpu.VMEM((CTX, lay.rows, lay.lanes), BF16),
            pltpu.VMEM((CTX - 1, lay.rows, lay.lanes), BF16),
            pltpu.VMEM((DP, lay.rows, lay.lanes), F32),
            dma((4, NC)), dma((NC,)), dma((NC,)), dma((NC,)), dma((NC,)),
            dma((CTX - 1,)), dma((CTX - 1,)), dma((Y - 1,)), dma((Y - 1,)), dma, dma,
            dma((NC,)), dma((NC,)), dma((Y - 1, NC // lay.batch)), dma((Y - 1, NC // lay.batch)),
            dma((CTX - 1,)), dma((CTX - 1,)), dma((DP - 1,)), dma((DP - 1,)),
        ],
        compiler_params=pltpu.CompilerParams(
            collective_id=0, has_side_effects=True, vmem_limit_bytes=60 * 2**20
        ),
        name="mixer",
    )(query_act, key_act, value_act, out_grad, filter_taps,
      doc_ids.reshape(-1, FL), jnp.asarray(fwd_tab), jnp.asarray(inv_tab))
    mixed, back = mixed.astype(F32), back.astype(F32)
    query_grad = (out_grad.astype(F32) * mixed).astype(BF16)
    key_grad = (back * value_act.astype(F32)).astype(BF16)
    value_grad = (back * key_act.astype(F32)).astype(BF16)
    return query_grad, key_grad, value_grad, filter_grad


def solution(mesh):
    act = P(("dp", "ctx"), None)
    return jax.shard_map(
        shards,
        mesh=mesh,
        in_specs=(act, act, act, act, P("ctx", None), P()),
        out_specs=(act, act, act, P("ctx", None)),
        check_vma=False,
    )
```

```python
import functools
import math

import jax
import jax.numpy as jnp
import numpy as np
import ml_dtypes
from jax import lax
from jax.experimental import pallas as pl
from jax.experimental.pallas import tpu as pltpu
from jax.sharding import PartitionSpec as P

FL = 128
BINS = 192
N = 2 * BINS
CHUNK = 256
F32 = jnp.float32
BF16 = jnp.bfloat16


def tables():
    k = np.arange(BINS)[:, None]
    fwd, inv = [], []
    for block in range(3):
        u = np.arange(FL)[None, :] + FL * block
        angle = np.pi * ((2 * k + 1) * u % (2 * N)) / N
        full = np.concatenate([np.cos(angle), np.sin(angle)], 0)
        high = full.astype(ml_dtypes.bfloat16)
        low = (full - high.astype(np.float64)).astype(ml_dtypes.bfloat16)
        fwd.append(np.concatenate([high, low], 1))
        inv.append(np.concatenate([high.T, low.T], 0))
    return np.stack(fwd), np.stack(inv[:2])


def forward(matrix, block):
    return jnp.dot(
        matrix, jnp.concatenate([block, block], 0), preferred_element_type=F32
    )


def inverse(matrix, cosines, sines):
    spectrum = jnp.concatenate([cosines, sines], 0).astype(BF16)
    both = jnp.dot(matrix, spectrum, preferred_element_type=F32)
    return both[:FL] + both[FL:]


def convolve(a, b):
    ca, sa, cb, sb = a[:BINS], a[BINS:], b[:BINS], b[BINS:]
    return ca * cb - sa * sb, ca * sb + sa * cb


def correlate(a, b):
    ca, sa, cb, sb = a[:BINS], a[BINS:], b[:BINS], b[BINS:]
    return ca * cb + sa * sb, ca * sb - sa * cb

MESH = pl.DeviceIdType.MESH


class Layout:
    def __init__(self, dp, ctx, chans, chunk=CHUNK):
        self.dp, self.ctx, self.cores, self.ys = dp, ctx, 2, dp // 2
        self.chans, self.chunk = chans, chunk
        self.chunks = chans // chunk
        self.half = self.chunks // 2
        self.batch = max(1, self.half // 4)
        self.rows = FL // dp
        self.lanes = chans // ctx


def remote(src, dst, send, recv, device):
    return pltpu.make_async_remote_copy(
        src_ref=src, dst_ref=dst, send_sem=send, recv_sem=recv, device_id=device,
        device_id_type=MESH,
    )


def kernel(lay, scale, q_hbm, k_hbm, v_hbm, o_hbm, taps, docs, fwd_tab, inv_tab,
           mixed_ref, back_ref, fg_ref,
           q, k, v, o, p, g, p_prev, g_next, mixed, back, pa_hat, ga_hat, pb_hat, gb_hat,
           e_own, e_prev, e_next, d_own, tap_own, tap_all, fg_part, c_recv, y_send, y_recv,
           x_own, x_send, x_recv, final,
           in_sem, out_sem, p_ssem, p_rsem, g_ssem, g_rsem, tx_ssem, tx_rsem,
           ty_ssem, ty_rsem, tc_ssem, tc_rsem, c_ssem, c_rsem, y_ssem, y_rsem,
           x_ssem, x_rsem, f_ssem, f_rsem):
    dp, ctx = lax.axis_index("dp"), lax.axis_index("ctx")
    DP, CTX, Y = lay.dp, lay.ctx, lay.ys
    NC, HALF, YB, CH = lay.chunks, lay.half, lay.batch, lay.chunk
    y, core = lax.div(dp, 2), lax.rem(dp, 2)
    me = dp * CTX + ctx
    after, before = lax.rem(me + 1, DP * CTX), lax.rem(me + DP * CTX - 1, DP * CTX)
    place = lambda flat: (lax.div(flat, CTX), lax.rem(flat, CTX))
    nxt, prv = place(after), place(before)
    c_peer = lambda r: (dp, lax.rem(ctx + r, CTX))
    y_peer = lambda r: (2 * lax.rem(y + r, Y) + core, ctx)
    d_peer = lambda r: (lax.rem(dp + r, DP), ctx)
    partner = (2 * y + 1 - core, ctx)
    slot = core * Y + y

    barrier = pltpu.get_barrier_semaphore()
    peers = [nxt, prv] + [d_peer(r) for r in range(1, DP)]
    for peer in peers:
        pl.semaphore_signal(barrier, inc=1, device_id=peer, device_id_type=MESH)

    def greet(r, carry):
        pl.semaphore_signal(barrier, inc=1, device_id=c_peer(r), device_id_type=MESH)
        return carry

    lax.fori_loop(1, CTX, greet, 0)

    def load(which, n):
        hbm, ref = ((q_hbm, q), (k_hbm, k), (v_hbm, v), (o_hbm, o))[which]
        return pltpu.make_async_copy(
            hbm.at[:, pl.ds(pl.multiple_of(n * CH, CH), CH)], ref.at[n], in_sem.at[which, n]
        )

    def start_loads(j, carry):
        for which, n in ((1, j), (2, j), (0, j + HALF), (3, j + HALF),
                         (1, j + HALF), (2, j + HALF), (0, j), (3, j)):
            load(which, n).start()
        return carry

    lax.fori_loop(0, HALF, start_loads, 0)

    turned = taps[...].T.astype(BF16)
    tap_own[...] = turned.reshape(DP, lay.rows, lay.lanes)
    tap_all[slot, ctx] = tap_own[slot]

    above, below = jnp.maximum(me - 1, 0), jnp.minimum(me + 1, DP * CTX - 1)
    own = docs[pl.ds(me, 1), :]
    first, last = own[:, :1], own[:, FL - 1 :]
    moved = (own != first).astype(F32)
    split = (first != last).astype(F32)
    keep_prev = (docs[pl.ds(above, 1), :] == first).astype(F32) * (me > 0).astype(F32)
    keep_next = (docs[pl.ds(below, 1), :] == last).astype(F32) * (me < DP * CTX - 1).astype(F32)
    twice = lambda row: jnp.concatenate([row, row], 1)
    t0, t1, t2 = (fwd_tab[i].astype(F32) for i in range(3))
    m = twice(moved)
    e_own[...] = (t0 * (1.0 - m) + t1 * m).astype(BF16)
    e_prev[...] = (-t2 * twice(keep_prev)).astype(BF16)
    e_next[...] = ((t1 * (1.0 - split) + t2 * split) * twice(keep_next)).astype(BF16)
    square = jnp.broadcast_to(moved, (FL, FL)).T
    wide = jnp.concatenate([square] * (N // FL), 1)
    for half in range(2):
        rows = pl.ds(half * FL, FL)
        d0, d1 = inv_tab[0, rows, :].astype(F32), inv_tab[1, rows, :].astype(F32)
        d_own[rows, :] = (d0 * (1.0 - wide) + d1 * wide).astype(BF16)

    def tap_ctx(r):
        here = tap_all.at[slot, ctx]
        return remote(here, here, tx_ssem.at[r - 1], tx_rsem.at[r - 1], c_peer(r))

    def tap_y(r):
        here = tap_all.at[slot]
        return remote(here, here, ty_ssem.at[r - 1], ty_rsem.at[r - 1], y_peer(r))

    def tap_c():
        here = tap_all.at[pl.ds(core * Y, Y)]
        return remote(here, here, tc_ssem, tc_rsem, partner)

    def halo_p(n):
        return remote(p.at[n], p_prev.at[n], p_ssem.at[n], p_rsem.at[n], nxt)

    def halo_g(n):
        return remote(g.at[n], g_next.at[n], g_ssem.at[n], g_rsem.at[n], prv)

    def pair(n):
        return remote(fg_part.at[n, 1 - core], c_recv.at[n], c_ssem.at[n], c_rsem.at[n], partner)

    def part_y(r, group):
        chunks = pl.ds(group * YB, YB)
        return remote(y_send.at[lax.rem(y + r, Y), chunks], y_recv.at[r - 1, chunks],
                      y_ssem.at[r - 1, group], y_rsem.at[r - 1, group], y_peer(r))

    def part_ctx(r):
        return remote(x_send.at[lax.rem(ctx + r, CTX)], x_recv.at[r - 1],
                      x_ssem.at[r - 1], x_rsem.at[r - 1], c_peer(r))

    def each_peer(action):
        def body(r, carry):
            action(r)
            return carry

        lax.fori_loop(1, CTX, body, 0)

    def part_f(r):
        here = final.at[slot]
        return remote(here, here, f_ssem.at[r - 1], f_rsem.at[r - 1], d_peer(r))

    def produce(j):
        for n in (j, j + HALF):
            load(1, n).wait()
            load(2, n).wait()
            p[n] = (k[n].astype(F32) * v[n].astype(F32)).astype(BF16)
            load(0, n).wait()
            load(3, n).wait()
            g[n] = (q[n].astype(F32) * o[n].astype(F32)).astype(BF16)

    def send(n):
        halo_p(n).start()
        halo_g(lax.rem(n + HALF, NC)).start()

    def produce_and_send(j, carry):
        produce(j)
        send(j)
        return carry

    def send_rest(n, carry):
        send(n)
        return carry

    produce(0)
    pl.semaphore_wait(barrier, len(peers) + CTX - 1)
    each_peer(lambda r: tap_ctx(r).start())
    send(0)
    lax.fori_loop(1, HALF, produce_and_send, 0)
    lax.fori_loop(HALF, NC, send_rest, 0)

    def absorb(n):
        pair(n).wait_recv()
        y_send[:, n] = (fg_part[n, core] + c_recv[n]).astype(BF16)

    def send_groups(gi):
        for group in (gi, gi + HALF // YB):
            for r in range(1, Y):
                part_y(r, group).start()

    def relay_y():
        each_peer(lambda r: tap_ctx(r).wait_recv())
        for r in range(1, Y):
            tap_y(r).start()

    def relay_c():
        for r in range(1, Y):
            tap_y(r).wait_recv()
        tap_c().start()

    def sum_y():
        for r in range(1, Y):
            for group in range(NC // YB):
                part_y(r, group).wait_recv()
        total = fg_part[:, core, y] + c_recv[:, y]
        for r in range(1, Y):
            total = total + y_recv[r - 1].astype(F32)
        per = CH // lay.lanes
        for i in range(CTX):
            lane = (i % per) * lay.lanes
            piece = total[i // per, :, lane : lane + lay.lanes]
            x_own[i] = piece
            x_send[i] = piece.astype(BF16)
        each_peer(lambda r: part_ctx(r).start())

    def sum_ctx():
        each_peer(lambda r: part_ctx(r).wait_recv())
        final[slot] = x_own[ctx] + jnp.sum(x_recv[...].astype(F32), axis=0)
        for r in range(1, DP):
            part_f(r).start()

    def scheduled(j, events):
        for step, event in events:
            if step < HALF:
                pl.when(j == step)(event)

    early = ((0, relay_y), (min(5, HALF - 1), relay_c))
    late = ((4, sum_y), (HALF, sum_ctx))

    def first_half(j, carry):
        scheduled(j, early)
        a, b = j, j + HALF
        halo_p(a).wait_recv()
        halo_g(b).wait_recv()
        ga = forward(e_own[...], g[a])
        pb = forward(e_own[...], p[b])
        pa = forward(e_own[...], p[a]) + forward(e_prev[...], p_prev[a])
        gb = forward(e_own[...], g[b]) + forward(e_next[...], g_next[b])
        ga_hat[j] = ga
        pb_hat[j] = pb
        pa_hat[j] = pa
        gb_hat[j] = gb
        fg_part[a] = inverse(inv_tab[0], *correlate(pa, ga)).reshape(2, Y, lay.rows, CH)
        fg_part[b] = inverse(inv_tab[0], *correlate(pb, gb)).reshape(2, Y, lay.rows, CH)
        pair(a).start()
        pair(b).start()

        @pl.when(j > 0)
        def _():
            absorb(j - 1)
            absorb(j - 1 + HALF)

        @pl.when((j > 0) & (lax.rem(j, YB) == 0))
        def _():
            send_groups(lax.div(j, YB) - 1)

        return carry

    lax.fori_loop(0, HALF, first_half, 0)
    absorb(HALF - 1)
    absorb(NC - 1)
    send_groups(HALF // YB - 1)
    tap_c().wait_recv()

    def taps_of(n):
        per = CH // lay.lanes
        return jnp.concatenate(
            [tap_all[:, n * per + i].reshape(FL, lay.lanes) for i in range(per)], 1
        )

    def write(ref, n, value):
        ref[n] = (value * (1.0 / BINS)).astype(BF16)

    def store(which, n):
        ref, hbm = ((mixed, mixed_ref), (back, back_ref))[which]
        return pltpu.make_async_copy(
            ref.at[n], hbm.at[:, pl.ds(pl.multiple_of(n * CH, CH), CH)], out_sem.at[which, n]
        )

    def second_half(j, carry):
        scheduled(j, late)
        a, b = j, j + HALF
        halo_g(a).wait_recv()
        halo_p(b).wait_recv()
        ha = forward(fwd_tab[0], taps_of(a))
        hb = forward(fwd_tab[0], taps_of(b))
        ga = ga_hat[j] + forward(e_next[...], g_next[a])
        pb = pb_hat[j] + forward(e_prev[...], p_prev[b])
        write(mixed, a, inverse(d_own[...], *convolve(ha, pa_hat[j])))
        write(back, a, inverse(d_own[...], *correlate(ha, ga)))
        write(mixed, b, inverse(d_own[...], *convolve(hb, pb)))
        write(back, b, inverse(d_own[...], *correlate(hb, gb_hat[j])))
        for n in (a, b):
            store(0, n).start()
            store(1, n).start()
        return carry

    lax.fori_loop(0, HALF, second_half, 0)
    for step, event in late:
        if step >= HALF:
            event()
    for r in range(1, DP):
        part_f(r).wait_recv()
    fg_ref[...] = final[...].reshape(FL, lay.lanes).T * (scale / BINS)

    def drain(n, carry):
        halo_p(n).wait_send()
        halo_g(n).wait_send()
        pair(n).wait_send()
        store(0, n).wait()
        store(1, n).wait()
        return carry

    lax.fori_loop(0, NC, drain, 0)
    each_peer(lambda r: tap_ctx(r).wait_send())
    each_peer(lambda r: part_ctx(r).wait_send())
    for r in range(1, Y):
        tap_y(r).wait_send()
        for group in range(NC // YB):
            part_y(r, group).wait_send()
    for r in range(1, DP):
        part_f(r).wait_send()
    tap_c().wait_send()


def shards(query_act, key_act, value_act, out_grad, filter_taps, doc_ids):
    rows, chans = key_act.shape
    lay = Layout(lax.axis_size("dp"), lax.axis_size("ctx"), chans)
    scale = 1.0 / math.sqrt(doc_ids.shape[0])
    fwd_tab, inv_tab = tables()
    acts = jax.ShapeDtypeStruct((rows, chans), BF16)
    any_spec, vmem = pl.BlockSpec(memory_space=pl.ANY), pl.BlockSpec(memory_space=pltpu.VMEM)
    NC, CH, CTX, DP, Y = lay.chunks, lay.chunk, lay.ctx, lay.dp, lay.ys
    block = pltpu.VMEM((NC, FL, CH), BF16)
    spectra = pltpu.VMEM((lay.half, N, CH), F32)
    mat = pltpu.VMEM((N, 2 * FL), BF16)
    dma = pltpu.SemaphoreType.DMA
    mixed, back, filter_grad = pl.pallas_call(
        functools.partial(kernel, lay, scale),
        in_specs=[any_spec] * 4 + [vmem] * 4,
        out_specs=[any_spec, any_spec, vmem],
        out_shape=[acts, acts, jax.ShapeDtypeStruct(filter_taps.shape, F32)],
        scratch_shapes=[block] * 10 + [spectra] * 4 + [
            mat, mat, mat,
            pltpu.VMEM((2 * FL, N), BF16),
            pltpu.VMEM((DP, lay.rows, lay.lanes), BF16),
            pltpu.VMEM((DP, CTX, lay.rows, lay.lanes), BF16),
            pltpu.VMEM((NC, 2, Y, lay.rows, CH), F32),
            pltpu.VMEM((NC, Y, lay.rows, CH), F32),
            pltpu.VMEM((Y, NC, lay.rows, CH), BF16),
            pltpu.VMEM((Y - 1, NC, lay.rows, CH), BF16),
            pltpu.VMEM((CTX, lay.rows, lay.lanes), F32),
            pltpu.VMEM((CTX, lay.rows, lay.lanes), BF16),
            pltpu.VMEM((CTX - 1, lay.rows, lay.lanes), BF16),
            pltpu.VMEM((DP, lay.rows, lay.lanes), F32),
            dma((4, NC)), dma((2, NC)), dma((NC,)), dma((NC,)), dma((NC,)), dma((NC,)),
            dma((CTX - 1,)), dma((CTX - 1,)), dma((Y - 1,)), dma((Y - 1,)), dma, dma,
            dma((NC,)), dma((NC,)), dma((Y - 1, NC // lay.batch)), dma((Y - 1, NC // lay.batch)),
            dma((CTX - 1,)), dma((CTX - 1,)), dma((DP - 1,)), dma((DP - 1,)),
        ],
        compiler_params=pltpu.CompilerParams(
            collective_id=0, has_side_effects=True, vmem_limit_bytes=44 * 2**20
        ),
        name="mixer",
    )(query_act, key_act, value_act, out_grad, filter_taps,
      doc_ids.reshape(-1, FL), jnp.asarray(fwd_tab), jnp.asarray(inv_tab))
    mixed, back = mixed.astype(F32), back.astype(F32)
    query_grad = (out_grad.astype(F32) * mixed).astype(BF16)
    key_grad = (back * value_act.astype(F32)).astype(BF16)
    value_grad = (back * key_act.astype(F32)).astype(BF16)
    return query_grad, key_grad, value_grad, filter_grad


def solution(mesh):
    act = P(("dp", "ctx"), None)
    return jax.shard_map(
        shards,
        mesh=mesh,
        in_specs=(act, act, act, act, P("ctx", None), P()),
        out_specs=(act, act, act, P("ctx", None)),
        check_vma=False,
    )
```

```python
import functools
import math

import jax
import jax.numpy as jnp
import numpy as np
import ml_dtypes
from jax import lax
from jax.experimental import pallas as pl
from jax.experimental.pallas import tpu as pltpu
from jax.sharding import PartitionSpec as P

FL = 128
BINS = 192
N = 2 * BINS
CHUNK = 256
F32 = jnp.float32
BF16 = jnp.bfloat16


def tables():
    k = np.arange(BINS)[:, None]
    fwd, inv = [], []
    for block in range(3):
        u = np.arange(FL)[None, :] + FL * block
        angle = np.pi * ((2 * k + 1) * u % (2 * N)) / N
        full = np.concatenate([np.cos(angle), np.sin(angle)], 0)
        high = full.astype(ml_dtypes.bfloat16)
        low = (full - high.astype(np.float64)).astype(ml_dtypes.bfloat16)
        fwd.append(np.concatenate([high, low], 1))
        inv.append(np.concatenate([high.T, low.T], 0))
    return np.stack(fwd), np.stack(inv[:2])


def forward(matrix, block):
    return jnp.dot(
        matrix, jnp.concatenate([block, block], 0), preferred_element_type=F32
    )


def inverse(matrix, cosines, sines):
    spectrum = jnp.concatenate([cosines, sines], 0).astype(BF16)
    both = jnp.dot(matrix, spectrum, preferred_element_type=F32)
    return both[:FL] + both[FL:]


def convolve(a, b):
    ca, sa, cb, sb = a[:BINS], a[BINS:], b[:BINS], b[BINS:]
    return ca * cb - sa * sb, ca * sb + sa * cb


def correlate(a, b):
    ca, sa, cb, sb = a[:BINS], a[BINS:], b[:BINS], b[BINS:]
    return ca * cb + sa * sb, ca * sb - sa * cb

MESH = pl.DeviceIdType.MESH


class Layout:
    def __init__(self, dp, ctx, chans, chunk=CHUNK):
        self.dp, self.ctx, self.cores, self.ys = dp, ctx, 2, dp // 2
        self.chans, self.chunk = chans, chunk
        self.chunks = chans // chunk
        self.half = self.chunks // 2
        self.batch = max(1, self.half // 4)
        self.rows = FL // dp
        self.lanes = chans // ctx


def remote(src, dst, send, recv, device):
    return pltpu.make_async_remote_copy(
        src_ref=src, dst_ref=dst, send_sem=send, recv_sem=recv, device_id=device,
        device_id_type=MESH,
    )


def kernel(lay, scale, q_hbm, k_hbm, v_hbm, o_hbm, taps_hbm, docs_hbm, fwd_hbm, inv_hbm,
           mixed_ref, back_ref, fg_ref,
           taps, docs, fwd_tab, inv_tab, q, k, v, o, p, g, p_prev, g_next, mixed, back, pa_hat, ga_hat, pb_hat, gb_hat,
           e_own, e_prev, e_next, d_own, tap_own, tap_all, fg_part, c_recv, y_send, y_recv,
           x_own, x_send, x_recv, final,
           small_sem, in_sem, out_sem, p_ssem, p_rsem, g_ssem, g_rsem, tx_ssem, tx_rsem,
           ty_ssem, ty_rsem, tc_ssem, tc_rsem, c_ssem, c_rsem, y_ssem, y_rsem,
           x_ssem, x_rsem, f_ssem, f_rsem):
    dp, ctx = lax.axis_index("dp"), lax.axis_index("ctx")
    DP, CTX, Y = lay.dp, lay.ctx, lay.ys
    NC, HALF, YB, CH = lay.chunks, lay.half, lay.batch, lay.chunk
    y, core = lax.div(dp, 2), lax.rem(dp, 2)
    me = dp * CTX + ctx
    after, before = lax.rem(me + 1, DP * CTX), lax.rem(me + DP * CTX - 1, DP * CTX)
    place = lambda flat: (lax.div(flat, CTX), lax.rem(flat, CTX))
    nxt, prv = place(after), place(before)
    c_peer = lambda r: (dp, lax.rem(ctx + r, CTX))
    y_peer = lambda r: (2 * lax.rem(y + r, Y) + core, ctx)
    d_peer = lambda r: (lax.rem(dp + r, DP), ctx)
    partner = (2 * y + 1 - core, ctx)
    slot = core * Y + y

    barrier = pltpu.get_barrier_semaphore()
    peers = [nxt, prv] + [d_peer(r) for r in range(1, DP)]
    for peer in peers:
        pl.semaphore_signal(barrier, inc=1, device_id=peer, device_id_type=MESH)

    def greet(r, carry):
        pl.semaphore_signal(barrier, inc=1, device_id=c_peer(r), device_id_type=MESH)
        return carry

    lax.fori_loop(1, CTX, greet, 0)

    def load(which, n):
        hbm, ref = ((q_hbm, q), (k_hbm, k), (v_hbm, v), (o_hbm, o))[which]
        return pltpu.make_async_copy(
            hbm.at[:, pl.ds(pl.multiple_of(n * CH, CH), CH)], ref.at[n], in_sem.at[which, n]
        )

    def start_loads(j, carry):
        for which, n in ((1, j), (2, j), (0, j + HALF), (3, j + HALF),
                         (1, j + HALF), (2, j + HALF), (0, j), (3, j)):
            load(which, n).start()
        return carry

    small = [
        pltpu.make_async_copy(hbm, ref, small_sem.at[i])
        for i, (hbm, ref) in enumerate(
            ((taps_hbm, taps), (docs_hbm, docs), (fwd_hbm, fwd_tab), (inv_hbm, inv_tab))
        )
    ]
    small[0].start()
    lax.fori_loop(0, HALF, start_loads, 0)
    for copy in small[1:]:
        copy.start()
    small[0].wait()

    turned = taps[...].T.astype(BF16)
    tap_own[...] = turned.reshape(DP, lay.rows, lay.lanes)
    tap_all[slot, ctx] = tap_own[slot]

    def tap_ctx(r):
        here = tap_all.at[slot, ctx]
        return remote(here, here, tx_ssem.at[r - 1], tx_rsem.at[r - 1], c_peer(r))

    def tap_y(r):
        here = tap_all.at[slot]
        return remote(here, here, ty_ssem.at[r - 1], ty_rsem.at[r - 1], y_peer(r))

    def tap_c():
        here = tap_all.at[pl.ds(core * Y, Y)]
        return remote(here, here, tc_ssem, tc_rsem, partner)

    def halo_p(n):
        return remote(p.at[n], p_prev.at[n], p_ssem.at[n], p_rsem.at[n], nxt)

    def halo_g(n):
        return remote(g.at[n], g_next.at[n], g_ssem.at[n], g_rsem.at[n], prv)

    def pair(n):
        return remote(fg_part.at[n, 1 - core], c_recv.at[n], c_ssem.at[n], c_rsem.at[n], partner)

    def part_y(r, group):
        chunks = pl.ds(group * YB, YB)
        return remote(y_send.at[lax.rem(y + r, Y), chunks], y_recv.at[r - 1, chunks],
                      y_ssem.at[r - 1, group], y_rsem.at[r - 1, group], y_peer(r))

    def part_ctx(r):
        return remote(x_send.at[lax.rem(ctx + r, CTX)], x_recv.at[r - 1],
                      x_ssem.at[r - 1], x_rsem.at[r - 1], c_peer(r))

    def each_peer(action):
        def body(r, carry):
            action(r)
            return carry

        lax.fori_loop(1, CTX, body, 0)

    def part_f(r):
        here = final.at[slot]
        return remote(here, here, f_ssem.at[r - 1], f_rsem.at[r - 1], d_peer(r))

    def produce(j):
        for n in (j, j + HALF):
            load(1, n).wait()
            load(2, n).wait()
            p[n] = (k[n].astype(F32) * v[n].astype(F32)).astype(BF16)
            load(0, n).wait()
            load(3, n).wait()
            g[n] = (q[n].astype(F32) * o[n].astype(F32)).astype(BF16)

    def send(n):
        halo_p(n).start()
        halo_g(lax.rem(n + HALF, NC)).start()

    def produce_and_send(j, carry):
        produce(j)
        send(j)
        return carry

    def send_rest(n, carry):
        send(n)
        return carry

    produce(0)
    pl.semaphore_wait(barrier, len(peers) + CTX - 1)
    each_peer(lambda r: tap_ctx(r).start())
    send(0)
    lax.fori_loop(1, HALF, produce_and_send, 0)
    lax.fori_loop(HALF, NC, send_rest, 0)

    for copy in small[1:]:
        copy.wait()
    above, below = jnp.maximum(me - 1, 0), jnp.minimum(me + 1, DP * CTX - 1)
    own = docs[pl.ds(me, 1), :]
    first, last = own[:, :1], own[:, FL - 1 :]
    moved = (own != first).astype(F32)
    split = (first != last).astype(F32)
    keep_prev = (docs[pl.ds(above, 1), :] == first).astype(F32) * (me > 0).astype(F32)
    keep_next = (docs[pl.ds(below, 1), :] == last).astype(F32) * (me < DP * CTX - 1).astype(F32)
    twice = lambda row: jnp.concatenate([row, row], 1)
    t0, t1, t2 = (fwd_tab[i].astype(F32) for i in range(3))
    m = twice(moved)
    e_own[...] = (t0 * (1.0 - m) + t1 * m).astype(BF16)
    e_prev[...] = (-t2 * twice(keep_prev)).astype(BF16)
    e_next[...] = ((t1 * (1.0 - split) + t2 * split) * twice(keep_next)).astype(BF16)
    square = jnp.broadcast_to(moved, (FL, FL)).T
    wide = jnp.concatenate([square] * (N // FL), 1)
    for half in range(2):
        rows = pl.ds(half * FL, FL)
        d0, d1 = inv_tab[0, rows, :].astype(F32), inv_tab[1, rows, :].astype(F32)
        d_own[rows, :] = (d0 * (1.0 - wide) + d1 * wide).astype(BF16)

    def absorb(n):
        pair(n).wait_recv()
        y_send[:, n] = (fg_part[n, core] + c_recv[n]).astype(BF16)

    def send_groups(gi):
        for group in (gi, gi + HALF // YB):
            for r in range(1, Y):
                part_y(r, group).start()

    def relay_y():
        each_peer(lambda r: tap_ctx(r).wait_recv())
        for r in range(1, Y):
            tap_y(r).start()

    def relay_c():
        for r in range(1, Y):
            tap_y(r).wait_recv()
        tap_c().start()

    def sum_y():
        for r in range(1, Y):
            for group in range(NC // YB):
                part_y(r, group).wait_recv()
        total = fg_part[:, core, y] + c_recv[:, y]
        for r in range(1, Y):
            total = total + y_recv[r - 1].astype(F32)
        per = CH // lay.lanes
        for i in range(CTX):
            lane = (i % per) * lay.lanes
            piece = total[i // per, :, lane : lane + lay.lanes]
            x_own[i] = piece
            x_send[i] = piece.astype(BF16)
        each_peer(lambda r: part_ctx(r).start())

    def sum_ctx():
        each_peer(lambda r: part_ctx(r).wait_recv())
        final[slot] = x_own[ctx] + jnp.sum(x_recv[...].astype(F32), axis=0)
        for r in range(1, DP):
            part_f(r).start()

    def scheduled(j, events):
        for step, event in events:
            if step < HALF:
                pl.when(j == step)(event)

    early = ((0, relay_y), (min(5, HALF - 1), relay_c))
    late = ((4, sum_y), (HALF, sum_ctx))

    def first_half(j, carry):
        scheduled(j, early)
        a, b = j, j + HALF
        halo_p(a).wait_recv()
        halo_g(b).wait_recv()
        ga = forward(e_own[...], g[a])
        pb = forward(e_own[...], p[b])
        pa = forward(e_own[...], p[a]) + forward(e_prev[...], p_prev[a])
        gb = forward(e_own[...], g[b]) + forward(e_next[...], g_next[b])
        ga_hat[j] = ga
        pb_hat[j] = pb
        pa_hat[j] = pa
        gb_hat[j] = gb
        fg_part[a] = inverse(inv_tab[0], *correlate(pa, ga)).reshape(2, Y, lay.rows, CH)
        fg_part[b] = inverse(inv_tab[0], *correlate(pb, gb)).reshape(2, Y, lay.rows, CH)
        pair(a).start()
        pair(b).start()

        @pl.when(j > 0)
        def _():
            absorb(j - 1)
            absorb(j - 1 + HALF)

        @pl.when((j > 0) & (lax.rem(j, YB) == 0))
        def _():
            send_groups(lax.div(j, YB) - 1)

        return carry

    lax.fori_loop(0, HALF, first_half, 0)
    absorb(HALF - 1)
    absorb(NC - 1)
    send_groups(HALF // YB - 1)
    tap_c().wait_recv()

    def taps_of(n):
        per = CH // lay.lanes
        return jnp.concatenate(
            [tap_all[:, n * per + i].reshape(FL, lay.lanes) for i in range(per)], 1
        )

    def write(ref, n, value):
        ref[n] = (value * (1.0 / BINS)).astype(BF16)

    def store(which, n):
        ref, hbm = ((mixed, mixed_ref), (back, back_ref))[which]
        return pltpu.make_async_copy(
            ref.at[n], hbm.at[:, pl.ds(pl.multiple_of(n * CH, CH), CH)], out_sem.at[which, n]
        )

    def second_half(j, carry):
        scheduled(j, late)
        a, b = j, j + HALF
        halo_g(a).wait_recv()
        halo_p(b).wait_recv()
        ha = forward(fwd_tab[0], taps_of(a))
        hb = forward(fwd_tab[0], taps_of(b))
        ga = ga_hat[j] + forward(e_next[...], g_next[a])
        pb = pb_hat[j] + forward(e_prev[...], p_prev[b])
        write(mixed, a, inverse(d_own[...], *convolve(ha, pa_hat[j])))
        write(back, a, inverse(d_own[...], *correlate(ha, ga)))
        write(mixed, b, inverse(d_own[...], *convolve(hb, pb)))
        write(back, b, inverse(d_own[...], *correlate(hb, gb_hat[j])))
        for n in (a, b):
            store(0, n).start()
            store(1, n).start()
        return carry

    lax.fori_loop(0, HALF, second_half, 0)
    for step, event in late:
        if step >= HALF:
            event()
    for r in range(1, DP):
        part_f(r).wait_recv()
    fg_ref[...] = final[...].reshape(FL, lay.lanes).T * (scale / BINS)

    def drain(n, carry):
        halo_p(n).wait_send()
        halo_g(n).wait_send()
        pair(n).wait_send()
        store(0, n).wait()
        store(1, n).wait()
        return carry

    lax.fori_loop(0, NC, drain, 0)
    each_peer(lambda r: tap_ctx(r).wait_send())
    each_peer(lambda r: part_ctx(r).wait_send())
    for r in range(1, Y):
        tap_y(r).wait_send()
        for group in range(NC // YB):
            part_y(r, group).wait_send()
    for r in range(1, DP):
        part_f(r).wait_send()
    tap_c().wait_send()


def shards(query_act, key_act, value_act, out_grad, filter_taps, doc_ids):
    rows, chans = key_act.shape
    lay = Layout(lax.axis_size("dp"), lax.axis_size("ctx"), chans)
    scale = 1.0 / math.sqrt(doc_ids.shape[0])
    fwd_tab, inv_tab = tables()
    acts = jax.ShapeDtypeStruct((rows, chans), BF16)
    any_spec, vmem = pl.BlockSpec(memory_space=pl.ANY), pl.BlockSpec(memory_space=pltpu.VMEM)
    NC, CH, CTX, DP, Y = lay.chunks, lay.chunk, lay.ctx, lay.dp, lay.ys
    block = pltpu.VMEM((NC, FL, CH), BF16)
    spectra = pltpu.VMEM((lay.half, N, CH), F32)
    mat = pltpu.VMEM((N, 2 * FL), BF16)
    dma = pltpu.SemaphoreType.DMA
    mixed, back, filter_grad = pl.pallas_call(
        functools.partial(kernel, lay, scale),
        in_specs=[pl.BlockSpec(memory_space=pltpu.HBM)] * 8,
        out_specs=[any_spec, any_spec, vmem],
        out_shape=[acts, acts, jax.ShapeDtypeStruct(filter_taps.shape, F32)],
        scratch_shapes=[
            pltpu.VMEM(filter_taps.shape, F32),
            pltpu.VMEM((DP * CTX, FL), jnp.int32),
            pltpu.VMEM(fwd_tab.shape, BF16),
            pltpu.VMEM(inv_tab.shape, BF16),
        ] + [block] * 10 + [spectra] * 4 + [
            mat, mat, mat,
            pltpu.VMEM((2 * FL, N), BF16),
            pltpu.VMEM((DP, lay.rows, lay.lanes), BF16),
            pltpu.VMEM((DP, CTX, lay.rows, lay.lanes), BF16),
            pltpu.VMEM((NC, 2, Y, lay.rows, CH), F32),
            pltpu.VMEM((NC, Y, lay.rows, CH), F32),
            pltpu.VMEM((Y, NC, lay.rows, CH), BF16),
            pltpu.VMEM((Y - 1, NC, lay.rows, CH), BF16),
            pltpu.VMEM((CTX, lay.rows, lay.lanes), F32),
            pltpu.VMEM((CTX, lay.rows, lay.lanes), BF16),
            pltpu.VMEM((CTX - 1, lay.rows, lay.lanes), BF16),
            pltpu.VMEM((DP, lay.rows, lay.lanes), F32),
            dma((4,)), dma((4, NC)), dma((2, NC)), dma((NC,)), dma((NC,)), dma((NC,)), dma((NC,)),
            dma((CTX - 1,)), dma((CTX - 1,)), dma((Y - 1,)), dma((Y - 1,)), dma, dma,
            dma((NC,)), dma((NC,)), dma((Y - 1, NC // lay.batch)), dma((Y - 1, NC // lay.batch)),
            dma((CTX - 1,)), dma((CTX - 1,)), dma((DP - 1,)), dma((DP - 1,)),
        ],
        compiler_params=pltpu.CompilerParams(
            collective_id=0, has_side_effects=True, vmem_limit_bytes=44 * 2**20
        ),
        name="mixer",
    )(*(
        pltpu.with_memory_space_constraint(array, pltpu.HBM)
        for array in (query_act, key_act, value_act, out_grad, filter_taps,
                      doc_ids.reshape(-1, FL), jnp.asarray(fwd_tab), jnp.asarray(inv_tab))
    ))
    mixed, back = mixed.astype(F32), back.astype(F32)
    query_grad = (out_grad.astype(F32) * mixed).astype(BF16)
    key_grad = (back * value_act.astype(F32)).astype(BF16)
    value_grad = (back * key_act.astype(F32)).astype(BF16)
    return query_grad, key_grad, value_grad, filter_grad


def solution(mesh):
    act = P(("dp", "ctx"), None)
    return jax.shard_map(
        shards,
        mesh=mesh,
        in_specs=(act, act, act, act, P("ctx", None), P()),
        out_specs=(act, act, act, P("ctx", None)),
        check_vma=False,
    )
```

```python
import functools
import math

import jax
import jax.numpy as jnp
import numpy as np
import ml_dtypes
from jax import lax
from jax.experimental import pallas as pl
from jax.experimental.pallas import tpu as pltpu
from jax.sharding import PartitionSpec as P

FL = 128
BINS = 192
N = 2 * BINS
CHUNK = 256
F32 = jnp.float32
BF16 = jnp.bfloat16


def tables():
    k = np.arange(BINS)[:, None]
    fwd, inv = [], []
    for block in range(3):
        u = np.arange(FL)[None, :] + FL * block
        angle = np.pi * ((2 * k + 1) * u % (2 * N)) / N
        full = np.concatenate([np.cos(angle), np.sin(angle)], 0)
        high = full.astype(ml_dtypes.bfloat16)
        low = (full - high.astype(np.float64)).astype(ml_dtypes.bfloat16)
        fwd.append(np.concatenate([high, low], 1))
        inv.append(np.concatenate([high.T, low.T], 0))
    return np.stack(fwd), np.stack(inv[:2])


def forward(matrix, block):
    return jnp.dot(
        matrix, jnp.concatenate([block, block], 0), preferred_element_type=F32
    )


def inverse(matrix, cosines, sines):
    spectrum = jnp.concatenate([cosines, sines], 0).astype(BF16)
    both = jnp.dot(matrix, spectrum, preferred_element_type=F32)
    return both[:FL] + both[FL:]


def convolve(a, b):
    ca, sa, cb, sb = a[:BINS], a[BINS:], b[:BINS], b[BINS:]
    return ca * cb - sa * sb, ca * sb + sa * cb


def correlate(a, b):
    ca, sa, cb, sb = a[:BINS], a[BINS:], b[:BINS], b[BINS:]
    return ca * cb + sa * sb, ca * sb - sa * cb

MESH = pl.DeviceIdType.MESH


class Layout:
    def __init__(self, dp, ctx, chans, chunk=CHUNK):
        self.dp, self.ctx, self.cores, self.ys = dp, ctx, 2, dp // 2
        self.chans, self.chunk = chans, chunk
        self.chunks = chans // chunk
        self.half = self.chunks // 2
        self.batch = max(1, self.half // 4)
        self.sum_step = min(4, self.half - 1)
        self.held = min(3, self.half - self.sum_step)
        self.rows = FL // dp
        self.lanes = chans // ctx


def remote(src, dst, send, recv, device):
    return pltpu.make_async_remote_copy(
        src_ref=src, dst_ref=dst, send_sem=send, recv_sem=recv, device_id=device,
        device_id_type=MESH,
    )


def kernel(lay, scale, q_hbm, k_hbm, v_hbm, o_hbm, taps_hbm, docs_hbm, fwd_hbm, inv_hbm,
           mixed_ref, back_ref, fg_ref,
           taps, docs, fwd_tab, inv_tab, q, k, v, o, p, g, p_prev, g_next, mixed, back, pa_hat, ga_hat, pb_hat, gb_hat,
           e_own, e_prev, e_next, d_own, tap_own, tap_all, fg_part, c_recv, y_send, y_recv,
           x_own, x_send, x_recv, final,
           small_sem, in_sem, out_sem, p_ssem, p_rsem, g_ssem, g_rsem, tx_ssem, tx_rsem,
           ty_ssem, ty_rsem, tc_ssem, tc_rsem, c_ssem, c_rsem, y_ssem, y_rsem,
           x_ssem, x_rsem, f_ssem, f_rsem):
    dp, ctx = lax.axis_index("dp"), lax.axis_index("ctx")
    DP, CTX, Y = lay.dp, lay.ctx, lay.ys
    NC, HALF, YB, CH = lay.chunks, lay.half, lay.batch, lay.chunk
    y, core = lax.div(dp, 2), lax.rem(dp, 2)
    me = dp * CTX + ctx
    after, before = lax.rem(me + 1, DP * CTX), lax.rem(me + DP * CTX - 1, DP * CTX)
    place = lambda flat: (lax.div(flat, CTX), lax.rem(flat, CTX))
    nxt, prv = place(after), place(before)
    c_peer = lambda r: (dp, lax.rem(ctx + r, CTX))
    y_peer = lambda r: (2 * lax.rem(y + r, Y) + core, ctx)
    d_peer = lambda r: (lax.rem(dp + r, DP), ctx)
    partner = (2 * y + 1 - core, ctx)
    slot = core * Y + y

    barrier = pltpu.get_barrier_semaphore()
    peers = [nxt, prv] + [d_peer(r) for r in range(1, DP)]
    for peer in peers:
        pl.semaphore_signal(barrier, inc=1, device_id=peer, device_id_type=MESH)

    def greet(r, carry):
        pl.semaphore_signal(barrier, inc=1, device_id=c_peer(r), device_id_type=MESH)
        return carry

    lax.fori_loop(1, CTX, greet, 0)

    def load(which, n):
        hbm, ref = ((q_hbm, q), (k_hbm, k), (v_hbm, v), (o_hbm, o))[which]
        return pltpu.make_async_copy(
            hbm.at[:, pl.ds(pl.multiple_of(n * CH, CH), CH)], ref.at[n], in_sem.at[which, n]
        )

    def start_loads(j, carry):
        for which, n in ((1, j), (2, j), (0, j + HALF), (3, j + HALF),
                         (1, j + HALF), (2, j + HALF), (0, j), (3, j)):
            load(which, n).start()
        return carry

    small = [
        pltpu.make_async_copy(hbm, ref, small_sem.at[i])
        for i, (hbm, ref) in enumerate(
            ((taps_hbm, taps), (docs_hbm, docs), (fwd_hbm, fwd_tab), (inv_hbm, inv_tab))
        )
    ]
    small[0].start()
    lax.fori_loop(0, HALF, start_loads, 0)
    for copy in small[1:]:
        copy.start()
    small[0].wait()

    turned = taps[...].T.astype(BF16)
    tap_own[...] = turned.reshape(DP, lay.rows, lay.lanes)
    tap_all[slot, ctx] = tap_own[slot]

    def tap_ctx(r):
        here = tap_all.at[slot, ctx]
        return remote(here, here, tx_ssem.at[r - 1], tx_rsem.at[r - 1], c_peer(r))

    def tap_y(r):
        here = tap_all.at[slot]
        return remote(here, here, ty_ssem.at[r - 1], ty_rsem.at[r - 1], y_peer(r))

    def tap_c():
        here = tap_all.at[pl.ds(core * Y, Y)]
        return remote(here, here, tc_ssem, tc_rsem, partner)

    def halo_p(n):
        return remote(p.at[n], p_prev.at[n], p_ssem.at[n], p_rsem.at[n], nxt)

    def halo_g(n):
        return remote(g.at[n], g_next.at[n], g_ssem.at[n], g_rsem.at[n], prv)

    def pair(n):
        return remote(fg_part.at[n, 1 - core], c_recv.at[n], c_ssem.at[n], c_rsem.at[n], partner)

    def part_y(r, group):
        chunks = pl.ds(group * YB, YB)
        return remote(y_send.at[lax.rem(y + r, Y), chunks], y_recv.at[r - 1, chunks],
                      y_ssem.at[r - 1, group], y_rsem.at[r - 1, group], y_peer(r))

    def part_ctx(r):
        return remote(x_send.at[lax.rem(ctx + r, CTX)], x_recv.at[r - 1],
                      x_ssem.at[r - 1], x_rsem.at[r - 1], c_peer(r))

    def each_peer(action):
        def body(r, carry):
            action(r)
            return carry

        lax.fori_loop(1, CTX, body, 0)

    def part_f(r):
        here = final.at[slot]
        return remote(here, here, f_ssem.at[r - 1], f_rsem.at[r - 1], d_peer(r))

    def produce(j):
        for n in (j, j + HALF):
            load(1, n).wait()
            load(2, n).wait()
            p[n] = (k[n].astype(F32) * v[n].astype(F32)).astype(BF16)
            load(0, n).wait()
            load(3, n).wait()
            g[n] = (q[n].astype(F32) * o[n].astype(F32)).astype(BF16)

    def send(n):
        halo_p(n).start()
        halo_g(lax.rem(n + HALF, NC)).start()

    def produce_and_send(j, carry):
        produce(j)
        send(j)
        return carry

    def send_rest(n, carry):
        send(n)
        return carry

    produce(0)
    pl.semaphore_wait(barrier, len(peers) + CTX - 1)
    each_peer(lambda r: tap_ctx(r).start())
    send(0)
    lax.fori_loop(1, HALF, produce_and_send, 0)
    lax.fori_loop(HALF, NC - lay.held, send_rest, 0)

    for copy in small[1:]:
        copy.wait()
    above, below = jnp.maximum(me - 1, 0), jnp.minimum(me + 1, DP * CTX - 1)
    own = docs[pl.ds(me, 1), :]
    first, last = own[:, :1], own[:, FL - 1 :]
    moved = (own != first).astype(F32)
    split = (first != last).astype(F32)
    keep_prev = (docs[pl.ds(above, 1), :] == first).astype(F32) * (me > 0).astype(F32)
    keep_next = (docs[pl.ds(below, 1), :] == last).astype(F32) * (me < DP * CTX - 1).astype(F32)
    twice = lambda row: jnp.concatenate([row, row], 1)
    t0, t1, t2 = (fwd_tab[i].astype(F32) for i in range(3))
    m = twice(moved)
    e_own[...] = (t0 * (1.0 - m) + t1 * m).astype(BF16)
    e_prev[...] = (-t2 * twice(keep_prev)).astype(BF16)
    e_next[...] = ((t1 * (1.0 - split) + t2 * split) * twice(keep_next)).astype(BF16)
    square = jnp.broadcast_to(moved, (FL, FL)).T
    wide = jnp.concatenate([square] * (N // FL), 1)
    for half in range(2):
        rows = pl.ds(half * FL, FL)
        d0, d1 = inv_tab[0, rows, :].astype(F32), inv_tab[1, rows, :].astype(F32)
        d_own[rows, :] = (d0 * (1.0 - wide) + d1 * wide).astype(BF16)

    def absorb(n):
        pair(n).wait_recv()
        y_send[:, n] = (fg_part[n, core] + c_recv[n]).astype(BF16)

    def send_groups(gi):
        for group in (gi, gi + HALF // YB):
            for r in range(1, Y):
                part_y(r, group).start()

    def relay_y():
        each_peer(lambda r: tap_ctx(r).wait_recv())
        for r in range(1, Y):
            tap_y(r).start()

    def relay_c():
        for r in range(1, Y):
            tap_y(r).wait_recv()
        tap_c().start()

    def sum_y():
        for r in range(1, Y):
            for group in range(NC // YB):
                part_y(r, group).wait_recv()
        total = fg_part[:, core, y] + c_recv[:, y]
        for r in range(1, Y):
            total = total + y_recv[r - 1].astype(F32)
        per = CH // lay.lanes
        for i in range(CTX):
            lane = (i % per) * lay.lanes
            piece = total[i // per, :, lane : lane + lay.lanes]
            x_own[i] = piece
            x_send[i] = piece.astype(BF16)
        each_peer(lambda r: part_ctx(r).start())
        lax.fori_loop(NC - lay.held, NC, send_rest, 0)

    def sum_ctx():
        each_peer(lambda r: part_ctx(r).wait_recv())
        final[slot] = x_own[ctx] + jnp.sum(x_recv[...].astype(F32), axis=0)
        for r in range(1, DP):
            part_f(r).start()

    def scheduled(j, events):
        for step, event in events:
            if step < HALF:
                pl.when(j == step)(event)

    early = ((0, relay_y), (min(5, HALF - 1), relay_c))
    late = ((lay.sum_step, sum_y), (HALF - 2 if HALF >= 8 else HALF, sum_ctx))

    def first_half(j, carry):
        scheduled(j, early)
        a, b = j, j + HALF
        halo_p(a).wait_recv()
        halo_g(b).wait_recv()
        ga = forward(e_own[...], g[a])
        pb = forward(e_own[...], p[b])
        pa = forward(e_own[...], p[a]) + forward(e_prev[...], p_prev[a])
        gb = forward(e_own[...], g[b]) + forward(e_next[...], g_next[b])
        ga_hat[j] = ga
        pb_hat[j] = pb
        pa_hat[j] = pa
        gb_hat[j] = gb
        fg_part[a] = inverse(inv_tab[0], *correlate(pa, ga)).reshape(2, Y, lay.rows, CH)
        fg_part[b] = inverse(inv_tab[0], *correlate(pb, gb)).reshape(2, Y, lay.rows, CH)
        pair(a).start()
        pair(b).start()

        @pl.when(j > 0)
        def _():
            absorb(j - 1)
            absorb(j - 1 + HALF)

        @pl.when((j > 0) & (lax.rem(j, YB) == 0))
        def _():
            send_groups(lax.div(j, YB) - 1)

        return carry

    lax.fori_loop(0, HALF, first_half, 0)
    absorb(HALF - 1)
    absorb(NC - 1)
    send_groups(HALF // YB - 1)
    tap_c().wait_recv()

    def taps_of(n):
        per = CH // lay.lanes
        return jnp.concatenate(
            [tap_all[:, n * per + i].reshape(FL, lay.lanes) for i in range(per)], 1
        )

    def write(ref, n, value):
        ref[n] = (value * (1.0 / BINS)).astype(BF16)

    def store(which, n):
        ref, hbm = ((mixed, mixed_ref), (back, back_ref))[which]
        return pltpu.make_async_copy(
            ref.at[n], hbm.at[:, pl.ds(pl.multiple_of(n * CH, CH), CH)], out_sem.at[which, n]
        )

    def second_half(j, carry):
        scheduled(j, late)
        a, b = j, j + HALF
        halo_g(a).wait_recv()
        halo_p(b).wait_recv()
        ha = forward(fwd_tab[0], taps_of(a))
        hb = forward(fwd_tab[0], taps_of(b))
        ga = ga_hat[j] + forward(e_next[...], g_next[a])
        pb = pb_hat[j] + forward(e_prev[...], p_prev[b])
        write(mixed, a, inverse(d_own[...], *convolve(ha, pa_hat[j])))
        write(back, a, inverse(d_own[...], *correlate(ha, ga)))
        write(mixed, b, inverse(d_own[...], *convolve(hb, pb)))
        write(back, b, inverse(d_own[...], *correlate(hb, gb_hat[j])))
        for n in (a, b):
            store(0, n).start()
            store(1, n).start()
        return carry

    lax.fori_loop(0, HALF, second_half, 0)
    for step, event in late:
        if step >= HALF:
            event()
    for r in range(1, DP):
        part_f(r).wait_recv()
    fg_ref[...] = final[...].reshape(FL, lay.lanes).T * (scale / BINS)

    def drain(n, carry):
        halo_p(n).wait_send()
        halo_g(n).wait_send()
        pair(n).wait_send()
        store(0, n).wait()
        store(1, n).wait()
        return carry

    lax.fori_loop(0, NC, drain, 0)
    each_peer(lambda r: tap_ctx(r).wait_send())
    each_peer(lambda r: part_ctx(r).wait_send())
    for r in range(1, Y):
        tap_y(r).wait_send()
        for group in range(NC // YB):
            part_y(r, group).wait_send()
    for r in range(1, DP):
        part_f(r).wait_send()
    tap_c().wait_send()


def shards(query_act, key_act, value_act, out_grad, filter_taps, doc_ids):
    rows, chans = key_act.shape
    lay = Layout(lax.axis_size("dp"), lax.axis_size("ctx"), chans)
    scale = 1.0 / math.sqrt(doc_ids.shape[0])
    fwd_tab, inv_tab = tables()
    acts = jax.ShapeDtypeStruct((rows, chans), BF16)
    any_spec, vmem = pl.BlockSpec(memory_space=pl.ANY), pl.BlockSpec(memory_space=pltpu.VMEM)
    NC, CH, CTX, DP, Y = lay.chunks, lay.chunk, lay.ctx, lay.dp, lay.ys
    block = pltpu.VMEM((NC, FL, CH), BF16)
    spectra = pltpu.VMEM((lay.half, N, CH), F32)
    mat = pltpu.VMEM((N, 2 * FL), BF16)
    dma = pltpu.SemaphoreType.DMA
    mixed, back, filter_grad = pl.pallas_call(
        functools.partial(kernel, lay, scale),
        in_specs=[pl.BlockSpec(memory_space=pltpu.HBM)] * 8,
        out_specs=[any_spec, any_spec, vmem],
        out_shape=[acts, acts, jax.ShapeDtypeStruct(filter_taps.shape, F32)],
        scratch_shapes=[
            pltpu.VMEM(filter_taps.shape, F32),
            pltpu.VMEM((DP * CTX, FL), jnp.int32),
            pltpu.VMEM(fwd_tab.shape, BF16),
            pltpu.VMEM(inv_tab.shape, BF16),
        ] + [block] * 10 + [spectra] * 4 + [
            mat, mat, mat,
            pltpu.VMEM((2 * FL, N), BF16),
            pltpu.VMEM((DP, lay.rows, lay.lanes), BF16),
            pltpu.VMEM((DP, CTX, lay.rows, lay.lanes), BF16),
            pltpu.VMEM((NC, 2, Y, lay.rows, CH), F32),
            pltpu.VMEM((NC, Y, lay.rows, CH), F32),
            pltpu.VMEM((Y, NC, lay.rows, CH), BF16),
            pltpu.VMEM((Y - 1, NC, lay.rows, CH), BF16),
            pltpu.VMEM((CTX, lay.rows, lay.lanes), F32),
            pltpu.VMEM((CTX, lay.rows, lay.lanes), BF16),
            pltpu.VMEM((CTX - 1, lay.rows, lay.lanes), BF16),
            pltpu.VMEM((DP, lay.rows, lay.lanes), F32),
            dma((4,)), dma((4, NC)), dma((2, NC)), dma((NC,)), dma((NC,)), dma((NC,)), dma((NC,)),
            dma((CTX - 1,)), dma((CTX - 1,)), dma((Y - 1,)), dma((Y - 1,)), dma, dma,
            dma((NC,)), dma((NC,)), dma((Y - 1, NC // lay.batch)), dma((Y - 1, NC // lay.batch)),
            dma((CTX - 1,)), dma((CTX - 1,)), dma((DP - 1,)), dma((DP - 1,)),
        ],
        compiler_params=pltpu.CompilerParams(
            collective_id=0, has_side_effects=True, vmem_limit_bytes=44 * 2**20
        ),
        name="mixer",
    )(*(
        pltpu.with_memory_space_constraint(array, pltpu.HBM)
        for array in (query_act, key_act, value_act, out_grad, filter_taps,
                      doc_ids.reshape(-1, FL), jnp.asarray(fwd_tab), jnp.asarray(inv_tab))
    ))
    mixed, back = mixed.astype(F32), back.astype(F32)
    query_grad = (out_grad.astype(F32) * mixed).astype(BF16)
    key_grad = (back * value_act.astype(F32)).astype(BF16)
    value_grad = (back * key_act.astype(F32)).astype(BF16)
    return query_grad, key_grad, value_grad, filter_grad


def solution(mesh):
    act = P(("dp", "ctx"), None)
    return jax.shard_map(
        shards,
        mesh=mesh,
        in_specs=(act, act, act, act, P("ctx", None), P()),
        out_specs=(act, act, act, P("ctx", None)),
        check_vma=False,
    )
```

```python
import functools
import math

import jax
import jax.numpy as jnp
import numpy as np
import ml_dtypes
from jax import lax
from jax.experimental import pallas as pl
from jax.experimental.pallas import tpu as pltpu
from jax.sharding import PartitionSpec as P

FL = 128
BINS = 192
N = 2 * BINS
CHUNK = 256
F32 = jnp.float32
BF16 = jnp.bfloat16


def tables():
    k = np.arange(BINS)[:, None]
    fwd, inv = [], []
    for block in range(3):
        u = np.arange(FL)[None, :] + FL * block
        angle = np.pi * ((2 * k + 1) * u % (2 * N)) / N
        full = np.concatenate([np.cos(angle), np.sin(angle)], 0)
        high = full.astype(ml_dtypes.bfloat16)
        low = (full - high.astype(np.float64)).astype(ml_dtypes.bfloat16)
        fwd.append(np.concatenate([high, low], 1))
        inv.append(np.concatenate([high.T, low.T], 0))
    return np.stack(fwd), np.stack(inv[:2])


def forward(matrix, block):
    return jnp.dot(
        matrix, jnp.concatenate([block, block], 0), preferred_element_type=F32
    )


def inverse(matrix, cosines, sines):
    spectrum = jnp.concatenate([cosines, sines], 0).astype(BF16)
    both = jnp.dot(matrix, spectrum, preferred_element_type=F32)
    return both[:FL] + both[FL:]


def convolve(a, b):
    ca, sa, cb, sb = a[:BINS], a[BINS:], b[:BINS], b[BINS:]
    return ca * cb - sa * sb, ca * sb + sa * cb


def correlate(a, b):
    ca, sa, cb, sb = a[:BINS], a[BINS:], b[:BINS], b[BINS:]
    return ca * cb + sa * sb, ca * sb - sa * cb

MESH = pl.DeviceIdType.MESH


class Layout:
    def __init__(self, dp, ctx, chans, chunk=CHUNK):
        self.dp, self.ctx, self.cores, self.ys = dp, ctx, 2, dp // 2
        self.chans, self.chunk = chans, chunk
        self.chunks = chans // chunk
        self.half = self.chunks // 2
        self.batch = max(1, self.half // 4)
        self.sum_step = min(6, self.half - 1)
        self.rows = FL // dp
        self.lanes = chans // ctx


def remote(src, dst, send, recv, device):
    return pltpu.make_async_remote_copy(
        src_ref=src, dst_ref=dst, send_sem=send, recv_sem=recv, device_id=device,
        device_id_type=MESH,
    )


def kernel(lay, scale, q_hbm, k_hbm, v_hbm, o_hbm, taps_hbm, docs_hbm, fwd_hbm, inv_hbm,
           qg_ref, kg_ref, vg_ref, fg_ref,
           taps, docs, fwd_tab, inv_tab, q, k, v, o, p, g, p_prev, g_next, qg, kg, vg, pa_hat, ga_hat, pb_hat, gb_hat,
           e_own, e_prev, e_next, d_own, tap_own, tap_all, fg_part, c_recv, y_send, y_recv,
           x_own, x_send, x_recv, final,
           small_sem, in_sem, out_sem, p_ssem, p_rsem, g_ssem, g_rsem, tx_ssem, tx_rsem,
           ty_ssem, ty_rsem, tc_ssem, tc_rsem, c_ssem, c_rsem, y_ssem, y_rsem,
           x_ssem, x_rsem, f_ssem, f_rsem):
    dp, ctx = lax.axis_index("dp"), lax.axis_index("ctx")
    DP, CTX, Y = lay.dp, lay.ctx, lay.ys
    NC, HALF, YB, CH = lay.chunks, lay.half, lay.batch, lay.chunk
    y, core = lax.div(dp, 2), lax.rem(dp, 2)
    me = dp * CTX + ctx
    after, before = lax.rem(me + 1, DP * CTX), lax.rem(me + DP * CTX - 1, DP * CTX)
    place = lambda flat: (lax.div(flat, CTX), lax.rem(flat, CTX))
    nxt, prv = place(after), place(before)
    c_peer = lambda r: (dp, lax.rem(ctx + r, CTX))
    y_peer = lambda r: (2 * lax.rem(y + r, Y) + core, ctx)
    d_peer = lambda r: (lax.rem(dp + r, DP), ctx)
    partner = (2 * y + 1 - core, ctx)
    slot = core * Y + y

    barrier = pltpu.get_barrier_semaphore()
    peers = [nxt, prv] + [d_peer(r) for r in range(1, DP)]
    for peer in peers:
        pl.semaphore_signal(barrier, inc=1, device_id=peer, device_id_type=MESH)

    def greet(r, carry):
        pl.semaphore_signal(barrier, inc=1, device_id=c_peer(r), device_id_type=MESH)
        return carry

    lax.fori_loop(1, CTX, greet, 0)

    def load(which, n):
        hbm, ref = ((q_hbm, q), (k_hbm, k), (v_hbm, v), (o_hbm, o))[which]
        return pltpu.make_async_copy(
            hbm.at[:, pl.ds(pl.multiple_of(n * CH, CH), CH)], ref.at[n], in_sem.at[which, n]
        )

    def start_loads(j, carry):
        for which, n in ((1, j), (2, j), (0, j + HALF), (3, j + HALF),
                         (1, j + HALF), (2, j + HALF), (0, j), (3, j)):
            load(which, n).start()
        return carry

    small = [
        pltpu.make_async_copy(hbm, ref, small_sem.at[i])
        for i, (hbm, ref) in enumerate(
            ((taps_hbm, taps), (docs_hbm, docs), (fwd_hbm, fwd_tab), (inv_hbm, inv_tab))
        )
    ]
    small[0].start()
    lax.fori_loop(0, HALF, start_loads, 0)
    for copy in small[1:]:
        copy.start()
    small[0].wait()

    turned = taps[...].T.astype(BF16)
    tap_own[...] = turned.reshape(DP, lay.rows, lay.lanes)
    tap_all[slot, ctx] = tap_own[slot]

    def tap_ctx(r):
        here = tap_all.at[slot, ctx]
        return remote(here, here, tx_ssem.at[r - 1], tx_rsem.at[r - 1], c_peer(r))

    def tap_y(r):
        here = tap_all.at[slot]
        return remote(here, here, ty_ssem.at[r - 1], ty_rsem.at[r - 1], y_peer(r))

    def tap_c():
        here = tap_all.at[pl.ds(core * Y, Y)]
        return remote(here, here, tc_ssem, tc_rsem, partner)

    def halo_p(n):
        return remote(p.at[n], p_prev.at[n], p_ssem.at[n], p_rsem.at[n], nxt)

    def halo_g(n):
        return remote(g.at[n], g_next.at[n], g_ssem.at[n], g_rsem.at[n], prv)

    def pair(n):
        return remote(fg_part.at[n, 1 - core], c_recv.at[n], c_ssem.at[n], c_rsem.at[n], partner)

    def part_y(r, group):
        chunks = pl.ds(group * YB, YB)
        return remote(y_send.at[lax.rem(y + r, Y), chunks], y_recv.at[r - 1, chunks],
                      y_ssem.at[r - 1, group], y_rsem.at[r - 1, group], y_peer(r))

    def part_ctx(r):
        return remote(x_send.at[lax.rem(ctx + r, CTX)], x_recv.at[r - 1],
                      x_ssem.at[r - 1], x_rsem.at[r - 1], c_peer(r))

    def each_peer(action):
        def body(r, carry):
            action(r)
            return carry

        lax.fori_loop(1, CTX, body, 0)

    def part_f(r):
        here = final.at[slot]
        return remote(here, here, f_ssem.at[r - 1], f_rsem.at[r - 1], d_peer(r))

    def produce(j):
        for n in (j, j + HALF):
            load(1, n).wait()
            load(2, n).wait()
            p[n] = (k[n].astype(F32) * v[n].astype(F32)).astype(BF16)
            load(0, n).wait()
            load(3, n).wait()
            g[n] = (q[n].astype(F32) * o[n].astype(F32)).astype(BF16)

    def send(n):
        halo_p(n).start()
        halo_g(lax.rem(n + HALF, NC)).start()

    def produce_and_send(j, carry):
        produce(j)
        send(j)
        return carry

    def send_rest(n, carry):
        send(n)
        return carry

    produce(0)
    pl.semaphore_wait(barrier, len(peers) + CTX - 1)
    each_peer(lambda r: tap_ctx(r).start())
    send(0)
    lax.fori_loop(1, HALF, produce_and_send, 0)
    lax.fori_loop(HALF, NC, send_rest, 0)

    for copy in small[1:]:
        copy.wait()
    above, below = jnp.maximum(me - 1, 0), jnp.minimum(me + 1, DP * CTX - 1)
    own = docs[pl.ds(me, 1), :]
    first, last = own[:, :1], own[:, FL - 1 :]
    moved = (own != first).astype(F32)
    split = (first != last).astype(F32)
    keep_prev = (docs[pl.ds(above, 1), :] == first).astype(F32) * (me > 0).astype(F32)
    keep_next = (docs[pl.ds(below, 1), :] == last).astype(F32) * (me < DP * CTX - 1).astype(F32)
    twice = lambda row: jnp.concatenate([row, row], 1)
    t0, t1, t2 = (fwd_tab[i].astype(F32) for i in range(3))
    m = twice(moved)
    e_own[...] = (t0 * (1.0 - m) + t1 * m).astype(BF16)
    e_prev[...] = (-t2 * twice(keep_prev)).astype(BF16)
    e_next[...] = ((t1 * (1.0 - split) + t2 * split) * twice(keep_next)).astype(BF16)
    square = jnp.broadcast_to(moved, (FL, FL)).T
    wide = jnp.concatenate([square] * (N // FL), 1)
    for half in range(2):
        rows = pl.ds(half * FL, FL)
        d0, d1 = inv_tab[0, rows, :].astype(F32), inv_tab[1, rows, :].astype(F32)
        d_own[rows, :] = (d0 * (1.0 - wide) + d1 * wide).astype(BF16)

    def absorb(n):
        pair(n).wait_recv()
        y_send[:, n] = (fg_part[n, core] + c_recv[n]).astype(BF16)

    def send_groups(gi):
        for group in (gi, gi + HALF // YB):
            for r in range(1, Y):
                part_y(r, group).start()

    def relay_y():
        each_peer(lambda r: tap_ctx(r).wait_recv())
        for r in range(1, Y):
            tap_y(r).start()

    def relay_c():
        for r in range(1, Y):
            tap_y(r).wait_recv()
        tap_c().start()

    def sum_y():
        for r in range(1, Y):
            for group in range(NC // YB):
                part_y(r, group).wait_recv()
        total = fg_part[:, core, y] + c_recv[:, y]
        for r in range(1, Y):
            total = total + y_recv[r - 1].astype(F32)
        per = CH // lay.lanes
        for i in range(CTX):
            lane = (i % per) * lay.lanes
            piece = total[i // per, :, lane : lane + lay.lanes]
            x_own[i] = piece
            x_send[i] = piece.astype(BF16)
        each_peer(lambda r: part_ctx(r).start())

    def sum_ctx():
        each_peer(lambda r: part_ctx(r).wait_recv())
        final[slot] = x_own[ctx] + jnp.sum(x_recv[...].astype(F32), axis=0)
        for r in range(1, DP):
            part_f(r).start()

    def scheduled(j, events):
        for step, event in events:
            if step < HALF:
                pl.when(j == step)(event)

    early = ((0, relay_y), (min(7, HALF - 1), relay_c))
    late = ((lay.sum_step, sum_y), (HALF, sum_ctx))

    def first_half(j, carry):
        scheduled(j, early)
        a, b = j, j + HALF
        halo_p(a).wait_recv()
        halo_g(b).wait_recv()
        ga = forward(e_own[...], g[a])
        pb = forward(e_own[...], p[b])
        pa = forward(e_own[...], p[a]) + forward(e_prev[...], p_prev[a])
        gb = forward(e_own[...], g[b]) + forward(e_next[...], g_next[b])
        ga_hat[j] = ga
        pb_hat[j] = pb
        pa_hat[j] = pa
        gb_hat[j] = gb
        fg_part[a] = inverse(inv_tab[0], *correlate(pa, ga)).reshape(2, Y, lay.rows, CH)
        fg_part[b] = inverse(inv_tab[0], *correlate(pb, gb)).reshape(2, Y, lay.rows, CH)
        pair(a).start()
        pair(b).start()

        @pl.when(j > 0)
        def _():
            absorb(j - 1)
            absorb(j - 1 + HALF)

        @pl.when((j > 0) & (lax.rem(j, YB) == 0))
        def _():
            send_groups(lax.div(j, YB) - 1)

        return carry

    lax.fori_loop(0, HALF, first_half, 0)
    absorb(HALF - 1)
    absorb(NC - 1)
    send_groups(HALF // YB - 1)
    tap_c().wait_recv()

    def taps_of(n):
        per = CH // lay.lanes
        return jnp.concatenate(
            [tap_all[:, n * per + i].reshape(FL, lay.lanes) for i in range(per)], 1
        )

    def rounded(value):
        return (value * (1.0 / BINS)).astype(BF16).astype(F32)

    def write_query(n, value):
        qg[n] = (o[n].astype(F32) * rounded(value)).astype(BF16)

    def write_kv(n, value):
        back = rounded(value)
        kg[n] = (back * v[n].astype(F32)).astype(BF16)
        vg[n] = (back * k[n].astype(F32)).astype(BF16)

    def store(which, n):
        ref, out = ((qg, qg_ref), (kg, kg_ref), (vg, vg_ref))[which]
        return pltpu.make_async_copy(
            ref.at[n], out.at[:, pl.ds(pl.multiple_of(n * CH, CH), CH)], out_sem.at[which, n]
        )

    def second_half(j, carry):
        scheduled(j, late)
        a, b = j, j + HALF
        halo_g(a).wait_recv()
        halo_p(b).wait_recv()
        ha = forward(fwd_tab[0], taps_of(a))
        hb = forward(fwd_tab[0], taps_of(b))
        ga = ga_hat[j] + forward(e_next[...], g_next[a])
        pb = pb_hat[j] + forward(e_prev[...], p_prev[b])
        write_query(a, inverse(d_own[...], *convolve(ha, pa_hat[j])))
        write_kv(a, inverse(d_own[...], *correlate(ha, ga)))
        write_query(b, inverse(d_own[...], *convolve(hb, pb)))
        write_kv(b, inverse(d_own[...], *correlate(hb, gb_hat[j])))
        for n in (a, b):
            for which in range(3):
                store(which, n).start()
        return carry

    lax.fori_loop(0, HALF, second_half, 0)
    for step, event in late:
        if step >= HALF:
            event()
    for r in range(1, DP):
        part_f(r).wait_recv()
    fg_ref[...] = final[...].reshape(FL, lay.lanes).T * (scale / BINS)

    def drain(n, carry):
        halo_p(n).wait_send()
        halo_g(n).wait_send()
        pair(n).wait_send()
        for which in range(3):
            store(which, n).wait()
        return carry

    lax.fori_loop(0, NC, drain, 0)
    each_peer(lambda r: tap_ctx(r).wait_send())
    each_peer(lambda r: part_ctx(r).wait_send())
    for r in range(1, Y):
        tap_y(r).wait_send()
        for group in range(NC // YB):
            part_y(r, group).wait_send()
    for r in range(1, DP):
        part_f(r).wait_send()
    tap_c().wait_send()


def put_out(*refs):
    sem = refs[8]
    copies = []
    for i in range(4):
        half = refs[i].shape[0] // 2
        for j in range(2):
            rows = pl.ds(j * half, half)
            copies.append(
                pltpu.make_async_copy(refs[i].at[rows], refs[4 + i].at[rows], sem.at[i, j])
            )
    for copy in copies:
        copy.start()
    for copy in copies:
        copy.wait()


def shards(query_act, key_act, value_act, out_grad, filter_taps, doc_ids):
    rows, chans = key_act.shape
    lay = Layout(lax.axis_size("dp"), lax.axis_size("ctx"), chans)
    scale = 1.0 / math.sqrt(doc_ids.shape[0])
    fwd_tab, inv_tab = tables()
    acts = jax.ShapeDtypeStruct((rows, chans), BF16)
    any_spec, vmem = pl.BlockSpec(memory_space=pl.ANY), pl.BlockSpec(memory_space=pltpu.VMEM)
    NC, CH, CTX, DP, Y = lay.chunks, lay.chunk, lay.ctx, lay.dp, lay.ys
    block = pltpu.VMEM((NC, FL, CH), BF16)
    spectra = pltpu.VMEM((lay.half, N, CH), F32)
    mat = pltpu.VMEM((N, 2 * FL), BF16)
    dma = pltpu.SemaphoreType.DMA
    results = pl.pallas_call(
        functools.partial(kernel, lay, scale),
        in_specs=[pl.BlockSpec(memory_space=pltpu.HBM)] * 8,
        out_specs=[any_spec] * 3 + [vmem],
        out_shape=[acts, acts, acts, jax.ShapeDtypeStruct(filter_taps.shape, F32)],
        scratch_shapes=[
            pltpu.VMEM(filter_taps.shape, F32),
            pltpu.VMEM((DP * CTX, FL), jnp.int32),
            pltpu.VMEM(fwd_tab.shape, BF16),
            pltpu.VMEM(inv_tab.shape, BF16),
        ] + [block] * 11 + [spectra] * 4 + [
            mat, mat, mat,
            pltpu.VMEM((2 * FL, N), BF16),
            pltpu.VMEM((DP, lay.rows, lay.lanes), BF16),
            pltpu.VMEM((DP, CTX, lay.rows, lay.lanes), BF16),
            pltpu.VMEM((NC, 2, Y, lay.rows, CH), F32),
            pltpu.VMEM((NC, Y, lay.rows, CH), F32),
            pltpu.VMEM((Y, NC, lay.rows, CH), BF16),
            pltpu.VMEM((Y - 1, NC, lay.rows, CH), BF16),
            pltpu.VMEM((CTX, lay.rows, lay.lanes), F32),
            pltpu.VMEM((CTX, lay.rows, lay.lanes), BF16),
            pltpu.VMEM((CTX - 1, lay.rows, lay.lanes), BF16),
            pltpu.VMEM((DP, lay.rows, lay.lanes), F32),
            dma((4,)), dma((4, NC)), dma((3, NC)), dma((NC,)), dma((NC,)), dma((NC,)), dma((NC,)),
            dma((CTX - 1,)), dma((CTX - 1,)), dma((Y - 1,)), dma((Y - 1,)), dma, dma,
            dma((NC,)), dma((NC,)), dma((Y - 1, NC // lay.batch)), dma((Y - 1, NC // lay.batch)),
            dma((CTX - 1,)), dma((CTX - 1,)), dma((DP - 1,)), dma((DP - 1,)),
        ],
        compiler_params=pltpu.CompilerParams(
            collective_id=0, has_side_effects=True, vmem_limit_bytes=44 * 2**20
        ),
        name="mixer",
    )(*(
        pltpu.with_memory_space_constraint(array, pltpu.HBM)
        for array in (query_act, key_act, value_act, out_grad, filter_taps,
                      doc_ids.reshape(-1, FL), jnp.asarray(fwd_tab), jnp.asarray(inv_tab))
    ))
    return pl.pallas_call(
        put_out,
        in_specs=[any_spec] * 4,
        out_specs=[any_spec] * 4,
        out_shape=[acts, acts, acts, jax.ShapeDtypeStruct(filter_taps.shape, F32)],
        scratch_shapes=[dma((4, 2))],
        compiler_params=pltpu.CompilerParams(vmem_limit_bytes=8 * 2**20),
        name="put_out",
    )(*results)


def solution(mesh):
    act = P(("dp", "ctx"), None)
    return jax.shard_map(
        shards,
        mesh=mesh,
        in_specs=(act, act, act, act, P("ctx", None), P()),
        out_specs=(act, act, act, P("ctx", None)),
        check_vma=False,
    )
```

```python
import functools
import math

import jax
import jax.numpy as jnp
import numpy as np
import ml_dtypes
from jax import lax
from jax.experimental import pallas as pl
from jax.experimental.pallas import tpu as pltpu
from jax.sharding import PartitionSpec as P

FL = 128
BINS = 192
N = 2 * BINS
CHUNK = 256
F32 = jnp.float32
BF16 = jnp.bfloat16


def tables():
    k = np.arange(BINS)[:, None]
    fwd, inv = [], []
    for block in range(3):
        u = np.arange(FL)[None, :] + FL * block
        angle = np.pi * ((2 * k + 1) * u % (2 * N)) / N
        full = np.concatenate([np.cos(angle), np.sin(angle)], 0)
        high = full.astype(ml_dtypes.bfloat16)
        low = (full - high.astype(np.float64)).astype(ml_dtypes.bfloat16)
        fwd.append(np.concatenate([high, low], 1))
        inv.append(np.concatenate([high.T, low.T], 0))
    return np.stack(fwd), np.stack(inv[:2])


def forward(matrix, block):
    return jnp.dot(
        matrix, jnp.concatenate([block, block], 0), preferred_element_type=F32
    )


def inverse(matrix, cosines, sines):
    spectrum = jnp.concatenate([cosines, sines], 0).astype(BF16)
    both = jnp.dot(matrix, spectrum, preferred_element_type=F32)
    return both[:FL] + both[FL:]


def convolve(a, b):
    ca, sa, cb, sb = a[:BINS], a[BINS:], b[:BINS], b[BINS:]
    return ca * cb - sa * sb, ca * sb + sa * cb


def correlate(a, b):
    ca, sa, cb, sb = a[:BINS], a[BINS:], b[:BINS], b[BINS:]
    return ca * cb + sa * sb, ca * sb - sa * cb

MESH = pl.DeviceIdType.MESH


class Layout:
    def __init__(self, dp, ctx, chans, chunk=CHUNK):
        self.dp, self.ctx, self.cores, self.ys = dp, ctx, 2, dp // 2
        self.chans, self.chunk = chans, chunk
        self.chunks = chans // chunk
        self.half = self.chunks // 2
        self.batch = max(1, self.half // 4)
        self.sum_step = min(6, self.half - 1)
        self.rows = FL // dp
        self.lanes = chans // ctx


def remote(src, dst, send, recv, device):
    return pltpu.make_async_remote_copy(
        src_ref=src, dst_ref=dst, send_sem=send, recv_sem=recv, device_id=device,
        device_id_type=MESH,
    )


def kernel(lay, scale, q_hbm, k_hbm, v_hbm, o_hbm, taps_hbm, docs_hbm, fwd_hbm, inv_hbm,
           qg_ref, kg_ref, vg_ref, fg_ref,
           taps, docs, fwd_tab, inv_tab, q, k, v, o, p, g, p_prev, g_next, qg, kg, vg, pa_hat, ga_hat, pb_hat, gb_hat,
           e_own, e_prev, e_next, d_own, tap_own, tap_all, fg_part, c_recv, y_send, y_recv,
           x_own, x_send, x_recv, final,
           small_sem, in_sem, out_sem, p_ssem, p_rsem, g_ssem, g_rsem, tx_ssem, tx_rsem,
           ty_ssem, ty_rsem, tc_ssem, tc_rsem, c_ssem, c_rsem, y_ssem, y_rsem,
           x_ssem, x_rsem, f_ssem, f_rsem):
    dp, ctx = lax.axis_index("dp"), lax.axis_index("ctx")
    DP, CTX, Y = lay.dp, lay.ctx, lay.ys
    NC, HALF, YB, CH = lay.chunks, lay.half, lay.batch, lay.chunk
    y, core = lax.div(dp, 2), lax.rem(dp, 2)
    me = dp * CTX + ctx
    after, before = lax.rem(me + 1, DP * CTX), lax.rem(me + DP * CTX - 1, DP * CTX)
    place = lambda flat: (lax.div(flat, CTX), lax.rem(flat, CTX))
    nxt, prv = place(after), place(before)
    c_peer = lambda r: (dp, lax.rem(ctx + r, CTX))
    y_peer = lambda r: (2 * lax.rem(y + r, Y) + core, ctx)
    d_peer = lambda r: (lax.rem(dp + r, DP), ctx)
    partner = (2 * y + 1 - core, ctx)
    slot = core * Y + y

    def load(which, n):
        hbm, ref = ((q_hbm, q), (k_hbm, k), (v_hbm, v), (o_hbm, o))[which]
        return pltpu.make_async_copy(
            hbm.at[:, pl.ds(pl.multiple_of(n * CH, CH), CH)], ref.at[n], in_sem.at[which, n]
        )

    def start_loads(j, carry):
        for which, n in ((1, j), (2, j), (0, j + HALF), (3, j + HALF),
                         (1, j + HALF), (2, j + HALF), (0, j), (3, j)):
            load(which, n).start()
        return carry

    small = [
        pltpu.make_async_copy(hbm, ref, small_sem.at[i])
        for i, (hbm, ref) in enumerate(
            ((taps_hbm, taps), (docs_hbm, docs), (fwd_hbm, fwd_tab), (inv_hbm, inv_tab))
        )
    ]
    start_loads(0, 0)
    small[0].start()
    barrier = pltpu.get_barrier_semaphore()
    peers = [nxt, prv] + [d_peer(r) for r in range(1, DP)]
    for peer in peers:
        pl.semaphore_signal(barrier, inc=1, device_id=peer, device_id_type=MESH)

    def greet(r, carry):
        pl.semaphore_signal(barrier, inc=1, device_id=c_peer(r), device_id_type=MESH)
        return carry

    lax.fori_loop(1, CTX, greet, 0)

    lax.fori_loop(1, HALF, start_loads, 0)
    for copy in small[1:]:
        copy.start()
    def tap_ctx(r):
        here = tap_all.at[slot, ctx]
        return remote(here, here, tx_ssem.at[r - 1], tx_rsem.at[r - 1], c_peer(r))

    def tap_y(r):
        here = tap_all.at[slot]
        return remote(here, here, ty_ssem.at[r - 1], ty_rsem.at[r - 1], y_peer(r))

    def tap_c():
        here = tap_all.at[pl.ds(core * Y, Y)]
        return remote(here, here, tc_ssem, tc_rsem, partner)

    def halo_p(n):
        return remote(p.at[n], p_prev.at[n], p_ssem.at[n], p_rsem.at[n], nxt)

    def halo_g(n):
        return remote(g.at[n], g_next.at[n], g_ssem.at[n], g_rsem.at[n], prv)

    def pair(n):
        return remote(fg_part.at[n, 1 - core], c_recv.at[n], c_ssem.at[n], c_rsem.at[n], partner)

    def part_y(r, group):
        chunks = pl.ds(group * YB, YB)
        return remote(y_send.at[lax.rem(y + r, Y), chunks], y_recv.at[r - 1, chunks],
                      y_ssem.at[r - 1, group], y_rsem.at[r - 1, group], y_peer(r))

    def part_ctx(r):
        return remote(x_send.at[lax.rem(ctx + r, CTX)], x_recv.at[r - 1],
                      x_ssem.at[r - 1], x_rsem.at[r - 1], c_peer(r))

    def each_peer(action):
        def body(r, carry):
            action(r)
            return carry

        lax.fori_loop(1, CTX, body, 0)

    def part_f(r):
        here = final.at[slot]
        return remote(here, here, f_ssem.at[r - 1], f_rsem.at[r - 1], d_peer(r))

    def produce(j):
        for n in (j, j + HALF):
            load(1, n).wait()
            load(2, n).wait()
            p[n] = (k[n].astype(F32) * v[n].astype(F32)).astype(BF16)
            load(0, n).wait()
            load(3, n).wait()
            g[n] = (q[n].astype(F32) * o[n].astype(F32)).astype(BF16)

    def send(n):
        halo_p(n).start()
        halo_g(lax.rem(n + HALF, NC)).start()

    def produce_and_send(j, carry):
        produce(j)
        send(j)
        return carry

    def send_rest(n, carry):
        send(n)
        return carry

    produce(0)
    pl.semaphore_wait(barrier, len(peers) + CTX - 1)
    send(0)
    small[0].wait()

    turned = taps[...].T.astype(BF16)
    tap_own[...] = turned.reshape(DP, lay.rows, lay.lanes)
    tap_all[slot, ctx] = tap_own[slot]
    each_peer(lambda r: tap_ctx(r).start())
    lax.fori_loop(1, HALF, produce_and_send, 0)
    lax.fori_loop(HALF, NC, send_rest, 0)

    for copy in small[1:]:
        copy.wait()
    above, below = jnp.maximum(me - 1, 0), jnp.minimum(me + 1, DP * CTX - 1)
    own = docs[pl.ds(me, 1), :]
    first, last = own[:, :1], own[:, FL - 1 :]
    moved = (own != first).astype(F32)
    split = (first != last).astype(F32)
    keep_prev = (docs[pl.ds(above, 1), :] == first).astype(F32) * (me > 0).astype(F32)
    keep_next = (docs[pl.ds(below, 1), :] == last).astype(F32) * (me < DP * CTX - 1).astype(F32)
    twice = lambda row: jnp.concatenate([row, row], 1)
    t0, t1, t2 = (fwd_tab[i].astype(F32) for i in range(3))
    m = twice(moved)
    e_own[...] = (t0 * (1.0 - m) + t1 * m).astype(BF16)
    e_prev[...] = (-t2 * twice(keep_prev)).astype(BF16)
    e_next[...] = ((t1 * (1.0 - split) + t2 * split) * twice(keep_next)).astype(BF16)
    square = jnp.broadcast_to(moved, (FL, FL)).T
    wide = jnp.concatenate([square] * (N // FL), 1)
    for half in range(2):
        rows = pl.ds(half * FL, FL)
        d0, d1 = inv_tab[0, rows, :].astype(F32), inv_tab[1, rows, :].astype(F32)
        d_own[rows, :] = (d0 * (1.0 - wide) + d1 * wide).astype(BF16)

    def absorb(n):
        pair(n).wait_recv()
        y_send[:, n] = (fg_part[n, core] + c_recv[n]).astype(BF16)

    def send_groups(gi):
        for group in (gi, gi + HALF // YB):
            for r in range(1, Y):
                part_y(r, group).start()

    def relay_y():
        each_peer(lambda r: tap_ctx(r).wait_recv())
        for r in range(1, Y):
            tap_y(r).start()

    def relay_c():
        for r in range(1, Y):
            tap_y(r).wait_recv()
        tap_c().start()

    def sum_y():
        for r in range(1, Y):
            for group in range(NC // YB):
                part_y(r, group).wait_recv()
        total = fg_part[:, core, y] + c_recv[:, y]
        for r in range(1, Y):
            total = total + y_recv[r - 1].astype(F32)
        per = CH // lay.lanes
        for i in range(CTX):
            lane = (i % per) * lay.lanes
            piece = total[i // per, :, lane : lane + lay.lanes]
            x_own[i] = piece
            x_send[i] = piece.astype(BF16)
        each_peer(lambda r: part_ctx(r).start())

    def sum_ctx():
        each_peer(lambda r: part_ctx(r).wait_recv())
        final[slot] = x_own[ctx] + jnp.sum(x_recv[...].astype(F32), axis=0)
        for r in range(1, DP):
            part_f(r).start()

    def scheduled(j, events):
        for step, event in events:
            if step < HALF:
                pl.when(j == step)(event)

    early = ((0, relay_y), (min(7, HALF - 1), relay_c))
    late = ((lay.sum_step, sum_y), (HALF, sum_ctx))

    def first_half(j, carry):
        scheduled(j, early)
        a, b = j, j + HALF
        halo_p(a).wait_recv()
        halo_g(b).wait_recv()
        ga = forward(e_own[...], g[a])
        pb = forward(e_own[...], p[b])
        pa = forward(e_own[...], p[a]) + forward(e_prev[...], p_prev[a])
        gb = forward(e_own[...], g[b]) + forward(e_next[...], g_next[b])
        ga_hat[j] = ga
        pb_hat[j] = pb
        pa_hat[j] = pa
        gb_hat[j] = gb
        fg_part[a] = inverse(inv_tab[0], *correlate(pa, ga)).reshape(2, Y, lay.rows, CH)
        fg_part[b] = inverse(inv_tab[0], *correlate(pb, gb)).reshape(2, Y, lay.rows, CH)
        pair(a).start()
        pair(b).start()

        @pl.when(j > 0)
        def _():
            absorb(j - 1)
            absorb(j - 1 + HALF)

        @pl.when((j > 0) & (lax.rem(j, YB) == 0))
        def _():
            send_groups(lax.div(j, YB) - 1)

        return carry

    lax.fori_loop(0, HALF, first_half, 0)
    absorb(HALF - 1)
    absorb(NC - 1)
    send_groups(HALF // YB - 1)
    tap_c().wait_recv()

    def taps_of(n):
        per = CH // lay.lanes
        return jnp.concatenate(
            [tap_all[:, n * per + i].reshape(FL, lay.lanes) for i in range(per)], 1
        )

    def rounded(value):
        return (value * (1.0 / BINS)).astype(BF16).astype(F32)

    def write_query(n, value):
        qg[n] = (o[n].astype(F32) * rounded(value)).astype(BF16)

    def write_kv(n, value):
        back = rounded(value)
        kg[n] = (back * v[n].astype(F32)).astype(BF16)
        vg[n] = (back * k[n].astype(F32)).astype(BF16)

    def store(which, n):
        ref, out = ((qg, qg_ref), (kg, kg_ref), (vg, vg_ref))[which]
        return pltpu.make_async_copy(
            ref.at[n], out.at[:, pl.ds(pl.multiple_of(n * CH, CH), CH)], out_sem.at[which, n]
        )

    def second_half(j, carry):
        scheduled(j, late)
        a, b = j, j + HALF
        halo_g(a).wait_recv()
        halo_p(b).wait_recv()
        ha = forward(fwd_tab[0], taps_of(a))
        hb = forward(fwd_tab[0], taps_of(b))
        ga = ga_hat[j] + forward(e_next[...], g_next[a])
        pb = pb_hat[j] + forward(e_prev[...], p_prev[b])
        write_query(a, inverse(d_own[...], *convolve(ha, pa_hat[j])))
        write_kv(a, inverse(d_own[...], *correlate(ha, ga)))
        write_query(b, inverse(d_own[...], *convolve(hb, pb)))
        write_kv(b, inverse(d_own[...], *correlate(hb, gb_hat[j])))
        for n in (a, b):
            for which in range(3):
                store(which, n).start()
        return carry

    lax.fori_loop(0, HALF, second_half, 0)
    for step, event in late:
        if step >= HALF:
            event()
    for r in range(1, DP):
        part_f(r).wait_recv()
    fg_ref[...] = final[...].reshape(FL, lay.lanes).T * (scale / BINS)

    def drain(n, carry):
        halo_p(n).wait_send()
        halo_g(n).wait_send()
        pair(n).wait_send()
        for which in range(3):
            store(which, n).wait()
        return carry

    lax.fori_loop(0, NC, drain, 0)
    each_peer(lambda r: tap_ctx(r).wait_send())
    each_peer(lambda r: part_ctx(r).wait_send())
    for r in range(1, Y):
        tap_y(r).wait_send()
        for group in range(NC // YB):
            part_y(r, group).wait_send()
    for r in range(1, DP):
        part_f(r).wait_send()
    tap_c().wait_send()


def put_out(*refs):
    sem = refs[8]
    copies = []
    for i in range(4):
        half = refs[i].shape[0] // 2
        for j in range(2):
            rows = pl.ds(j * half, half)
            copies.append(
                pltpu.make_async_copy(refs[i].at[rows], refs[4 + i].at[rows], sem.at[i, j])
            )
    for copy in copies:
        copy.start()
    for copy in copies:
        copy.wait()


def shards(query_act, key_act, value_act, out_grad, filter_taps, doc_ids):
    rows, chans = key_act.shape
    lay = Layout(lax.axis_size("dp"), lax.axis_size("ctx"), chans)
    scale = 1.0 / math.sqrt(doc_ids.shape[0])
    fwd_tab, inv_tab = tables()
    acts = jax.ShapeDtypeStruct((rows, chans), BF16)
    any_spec, vmem = pl.BlockSpec(memory_space=pl.ANY), pl.BlockSpec(memory_space=pltpu.VMEM)
    NC, CH, CTX, DP, Y = lay.chunks, lay.chunk, lay.ctx, lay.dp, lay.ys
    block = pltpu.VMEM((NC, FL, CH), BF16)
    spectra = pltpu.VMEM((lay.half, N, CH), F32)
    mat = pltpu.VMEM((N, 2 * FL), BF16)
    dma = pltpu.SemaphoreType.DMA
    results = pl.pallas_call(
        functools.partial(kernel, lay, scale),
        in_specs=[pl.BlockSpec(memory_space=pltpu.HBM)] * 8,
        out_specs=[any_spec] * 3 + [vmem],
        out_shape=[acts, acts, acts, jax.ShapeDtypeStruct(filter_taps.shape, F32)],
        scratch_shapes=[
            pltpu.VMEM(filter_taps.shape, F32),
            pltpu.VMEM((DP * CTX, FL), jnp.int32),
            pltpu.VMEM(fwd_tab.shape, BF16),
            pltpu.VMEM(inv_tab.shape, BF16),
        ] + [block] * 11 + [spectra] * 4 + [
            mat, mat, mat,
            pltpu.VMEM((2 * FL, N), BF16),
            pltpu.VMEM((DP, lay.rows, lay.lanes), BF16),
            pltpu.VMEM((DP, CTX, lay.rows, lay.lanes), BF16),
            pltpu.VMEM((NC, 2, Y, lay.rows, CH), F32),
            pltpu.VMEM((NC, Y, lay.rows, CH), F32),
            pltpu.VMEM((Y, NC, lay.rows, CH), BF16),
            pltpu.VMEM((Y - 1, NC, lay.rows, CH), BF16),
            pltpu.VMEM((CTX, lay.rows, lay.lanes), F32),
            pltpu.VMEM((CTX, lay.rows, lay.lanes), BF16),
            pltpu.VMEM((CTX - 1, lay.rows, lay.lanes), BF16),
            pltpu.VMEM((DP, lay.rows, lay.lanes), F32),
            dma((4,)), dma((4, NC)), dma((3, NC)), dma((NC,)), dma((NC,)), dma((NC,)), dma((NC,)),
            dma((CTX - 1,)), dma((CTX - 1,)), dma((Y - 1,)), dma((Y - 1,)), dma, dma,
            dma((NC,)), dma((NC,)), dma((Y - 1, NC // lay.batch)), dma((Y - 1, NC // lay.batch)),
            dma((CTX - 1,)), dma((CTX - 1,)), dma((DP - 1,)), dma((DP - 1,)),
        ],
        compiler_params=pltpu.CompilerParams(
            collective_id=0, has_side_effects=True, vmem_limit_bytes=44 * 2**20
        ),
        name="mixer",
    )(*(
        pltpu.with_memory_space_constraint(array, pltpu.HBM)
        for array in (query_act, key_act, value_act, out_grad, filter_taps,
                      doc_ids.reshape(-1, FL), jnp.asarray(fwd_tab), jnp.asarray(inv_tab))
    ))
    return pl.pallas_call(
        put_out,
        in_specs=[any_spec] * 4,
        out_specs=[any_spec] * 4,
        out_shape=[acts, acts, acts, jax.ShapeDtypeStruct(filter_taps.shape, F32)],
        scratch_shapes=[dma((4, 2))],
        compiler_params=pltpu.CompilerParams(vmem_limit_bytes=8 * 2**20),
        name="put_out",
    )(*results)


def solution(mesh):
    act = P(("dp", "ctx"), None)
    return jax.shard_map(
        shards,
        mesh=mesh,
        in_specs=(act, act, act, act, P("ctx", None), P()),
        out_specs=(act, act, act, P("ctx", None)),
        check_vma=False,
    )
```
